32 devices in a mesh: gx: 4 (over x, core), gy: 4 (over z), sa: 2 (over y).
Axes of the slice: x: 2, y: 2, z: 4, core: 2. Of those that a mesh axis runs over, the one named last changes fastest.
Arguments:
- slab: float32 [2, 64, 512, 512], P(None, 'sa', 'gx', 'gy'), may hold values from -30 to 30, as said below
- factor_x: float32 [512, 256], P('gx'), may hold values from -1 to 1, as said below
- factor_y: float32 [512, 256], P('gy'), may hold values from -1 to 1, as said below
Outputs:
- gram_x: float32 [512, 512], P(('gx', 'gy', 'sa'))
- gram_y: float32 [512, 512], P('gy')
- core: float32 [2, 64, 256, 256], P(None, 'sa', 'gx', 'gy')
The draws below stay inside these ranges and needn't reach their ends.
Inputs may be any that keep to these rules, and one draw needn't show every extreme that they name: `slab`: field values of a combustion state; rows of different x cells and species differ in scale. `factor_x`: the columns are orthonormal. `factor_y`: the columns are orthonormal.
All inputs are finite; a program needn't handle non-finite values.
Results may differ from the reference program's by a relative error of at most 0.000071.
Values sent between devices are 32-bit elements; how exact they have to be, the bound alone decides.
No kernel may reach another device: no remote copies, remote signals or barrier semaphores. Data moves between devices by JAX's collectives and lax.ppermute only.
A program may use at most 192 MiB of HBM per device.

```python
import math
import jax
import jax.numpy as jnp
from jax import lax

NX = 512
NY = 512
NS = 64
R = 256
NZ = 2


def draw_slab(key, part):
    keys = jax.random.split(jax.random.fold_in(key, 11), 3)
    low = math.log(0.3)
    high = math.log(3.0)
    row_scale = jnp.exp(jax.random.uniform(keys[0], (1, 1, NX, 1), minval=low, maxval=high))
    species_scale = jnp.exp(jax.random.uniform(keys[1], (1, NS, 1, 1), minval=low, maxval=high))
    base = jax.random.truncated_normal(keys[2], -4.0, 4.0, (NZ, NS, NX, NY))
    values = base * row_scale * species_scale
    return jnp.clip(values, -30.0, 30.0).astype(jnp.float32)


def draw_factor_x(key, part):
    matrix = jax.random.normal(jax.random.fold_in(key, 23), (NX, R))
    basis, upper = jnp.linalg.qr(matrix)
    return basis.astype(jnp.float32)


def draw_factor_y(key, part):
    matrix = jax.random.normal(jax.random.fold_in(key, 37), (NY, R))
    basis, upper = jnp.linalg.qr(matrix)
    return basis.astype(jnp.float32)


def setup_inputs(seed: int = 0) -> dict:
    seeds = jax.random.split(jax.random.key(seed), 4)
    return {
        "slab": draw_slab(jax.random.fold_in(seeds[3], 71), 0),
        "factor_x": draw_factor_x(jax.random.fold_in(seeds[3], 71), 0),
        "factor_y": draw_factor_y(jax.random.fold_in(seeds[3], 71), 0),
    }


def reference(slab, factor_x, factor_y):
    highest = lax.Precision.HIGHEST
    flat_x = jnp.transpose(slab, (2, 0, 1, 3)).reshape(NX, -1)
    gram_x = jnp.dot(flat_x.astype(jnp.float32), flat_x.T.astype(jnp.float32), precision=highest, preferred_element_type=jnp.float32) / (NY * NZ * NS)
    flat_y = jnp.transpose(slab, (3, 0, 1, 2)).reshape(NY, -1)
    gram_y = jnp.dot(flat_y.astype(jnp.float32), flat_y.T.astype(jnp.float32), precision=highest, preferred_element_type=jnp.float32) / (NX * NZ * NS)
    along_x = jnp.einsum('xa,zsxy->zsay', factor_x, slab, precision=highest)
    core = jnp.einsum('zsay,yb->zsab', along_x, factor_y, precision=highest)
    return (gram_x, gram_y, core)
```

```python
import jax
import jax.numpy as jnp
from jax import lax
from jax.sharding import PartitionSpec as P

HIGH = lax.Precision.HIGH
F32 = jnp.float32


def swap(value, axis, offset):
    size = lax.axis_size(axis)
    return lax.ppermute(value, axis, [(i, i ^ offset) for i in range(size)])


def far_first(size):
    return sorted(range(1, size), reverse=True)


def pick(value, index, axis):
    return lax.dynamic_index_in_dim(value, index, axis, keepdims=False)


def relabel(blocks, offset):
    return [blocks[o ^ offset] for o in range(len(blocks))]


def split_cols(value, count):
    width = value.shape[-1] // count
    return [value[..., o * width : (o + 1) * width] for o in range(count)]


def absolute_cols(value, count, me):
    blocks = jnp.stack(split_cols(value, count))
    return jnp.concatenate([pick(blocks, me ^ o, 0) for o in range(count)], axis=-1)


def shards(slab, factor_x, factor_y):
    z_cells, s_local, x_local, y_local = slab.shape
    nx, ny, ns = lax.axis_size("gx"), lax.axis_size("gy"), lax.axis_size("sa")
    me_x, me_y, me_s = lax.axis_index("gx"), lax.axis_index("gy"), lax.axis_index("sa")
    rank = factor_x.shape[1]
    a_block, b_block = rank // nx, rank // ny
    rows = z_cells * s_local
    flat = slab.reshape((rows, x_local, y_local))
    own_y, own_x = rows // ny, rows // nx
    chunks = 4
    n = own_y // chunks
    x_total, y_total, s_total = x_local * nx, y_local * ny, s_local * ns

    along_y = [[None] * ny for _ in range(chunks)]
    for c in range(chunks):
        for k in far_first(ny) + [0]:
            part = lax.dynamic_slice_in_dim(flat, (me_y ^ k) * own_y + c * n, n, 0)
            along_y[c][k] = swap(part, "gy", k) if k else part
    along_x = [None] * nx
    for k in far_first(nx) + [0]:
        part = lax.dynamic_slice_in_dim(flat, (me_x ^ k) * own_x, own_x, 0)
        along_x[k] = swap(part, "gx", k) if k else part

    piece = factor_y.reshape((nx, y_local // nx, rank))
    mine = pick(piece, me_x, 0)
    crossed = jnp.stack([swap(mine, "gy", k) for k in range(1, ny)])
    parts = [crossed] + [swap(crossed, "gx", k) for k in range(1, nx)]
    parts = jnp.stack(parts)
    ordered = jnp.stack([pick(parts, me_x ^ o, 0) for o in range(nx)])
    others = jnp.transpose(ordered, (1, 0, 2, 3)).reshape((ny - 1, y_local, rank))
    whole_fy = jnp.concatenate([factor_y[None], others], axis=0).reshape((ny * y_local, rank))
    fy_cols = whole_fy.reshape((ny * y_local, ny, b_block))
    whole_fy = jnp.concatenate([pick(fy_cols, me_y ^ q, 1) for q in range(ny)], axis=-1)
    fx_cols = factor_x.reshape((x_local, nx, a_block))
    local_fx = jnp.concatenate([pick(fx_cols, me_x ^ o, 1) for o in range(nx)], axis=-1)

    gy_sum = None
    core_parts = []
    for c in range(chunks):
        wide = jnp.concatenate(along_y[c], axis=-1).reshape((n * x_local, ny * y_local))
        term = lax.dot_general(
            wide, wide, (((0,), (0,)), ((), ())), precision=HIGH, preferred_element_type=F32
        )
        gy_sum = term if gy_sum is None else gy_sum + term
        half = jnp.dot(wide, whole_fy, precision=HIGH, preferred_element_type=F32)
        half = half.reshape((n, x_local, rank))
        full = jnp.einsum("xa,nxb->anb", local_fx, half, precision=HIGH, preferred_element_type=F32)
        blocks = full.reshape((nx, a_block, n, rank))
        bit = 1
        blocks = [blocks[o] for o in range(nx)]
        while bit < nx:
            keep = [o for o in range(len(blocks) * bit) if not o % (2 * bit)]
            table = dict(zip(range(0, nx, bit), blocks))
            sent = jnp.stack([table[o | bit] for o in keep])
            got = swap(sent, "gx", bit)
            blocks = [table[o] + got[i] for i, o in enumerate(keep)]
            bit *= 2
        done = blocks[0].reshape((a_block, n // 2, 2, ny, b_block))
        done = jnp.transpose(done, (3, 1, 0, 2, 4)).reshape((ny, n // 2, a_block, 2 * b_block))
        core_parts.append([swap(done[q], "gy", q) if q else done[q] for q in range(ny)])

    stack = jnp.stack([jnp.stack([core_parts[c][q] for c in range(chunks)]) for q in range(ny)])
    stack = jnp.stack([pick(stack, me_y ^ q, 0) for q in range(ny)])
    stack = stack.reshape((rows // 2, a_block, 2, b_block))
    core = jnp.transpose(stack, (0, 2, 1, 3)).reshape((z_cells, s_local, a_block, b_block))

    tall = jnp.concatenate(along_x, axis=1)
    gx_sum = jnp.einsum("rxy,rwy->xw", tall, tall, precision=HIGH, preferred_element_type=F32)
    table = {o: gx_sum[o * x_local : (o + 1) * x_local] for o in range(nx)}
    bit = 1
    while bit < nx:
        keep = [o for o in table if not o & bit]
        got = swap(jnp.stack([table[o | bit] for o in keep]), "gx", bit)
        got = jnp.concatenate(relabel(split_cols(got, nx), bit), axis=-1)
        table = {o: table[o] + got[i] for i, o in enumerate(keep)}
        bit *= 2
    out_rows = x_local // (ny * ns)
    own = table[0].reshape((ny, ns, out_rows, x_total))
    total = pick(own, me_s, 1)
    for k in range(1, ns):
        total = total + swap(pick(own, me_s ^ k, 1), "sa", k)
    gram_x = pick(total, me_y, 0)
    for k in range(1, ny):
        gram_x = gram_x + swap(pick(total, me_y ^ k, 0), "gy", k)
    gram_x = absolute_cols(gram_x, nx, me_x) / (y_total * z_cells * s_total)

    shard = y_local // (nx * ns)
    cur = gy_sum.reshape((ny, nx * ns * shard, y_total))
    bit = 1
    while bit < nx:
        cur = cur.reshape((ny, 2, -1, y_total))
        mybit = (me_x // bit) % 2
        cur = pick(cur, mybit, 1) + swap(pick(cur, 1 - mybit, 1), "gx", bit)
        bit *= 2
    cur = cur.reshape((ny, ns, shard, y_total))
    total = pick(cur, me_s, 1)
    for k in range(1, ns):
        total = total + swap(pick(cur, me_s ^ k, 1), "sa", k)
    row = total[0]
    for k in range(1, ny):
        got = swap(total[k], "gy", k)
        row = row + jnp.concatenate(relabel(split_cols(got, ny), k), axis=-1)
    row = absolute_cols(row, ny, me_y) / (x_total * z_cells * s_total)
    both = jnp.stack([row] + [swap(row, "sa", k) for k in range(1, ns)])
    cur = jnp.concatenate([pick(both, me_s ^ k, 0) for k in range(ns)], axis=0)
    bit = nx // 2
    while bit:
        got = swap(cur, "gx", bit)
        high = (me_x // bit) % 2 == 1
        cur = jnp.concatenate([jnp.where(high, got, cur), jnp.where(high, cur, got)], axis=0)
        bit //= 2
    return (gram_x, cur, core)


def solution(mesh):
    in_specs = (P(None, "sa", "gx", "gy"), P("gx", None), P("gy", None))
    out_specs = (P(("gx", "gy", "sa"), None), P("gy", None), P(None, "sa", "gx", "gy"))
    return jax.shard_map(shards, mesh=mesh, in_specs=in_specs, out_specs=out_specs, check_vma=False)
```

```python
import functools

import jax
import jax.numpy as jnp
from jax import lax
from jax.experimental import pallas as pl
from jax.experimental.pallas import tpu as pltpu
from jax.sharding import PartitionSpec as P


CHUNKS = 4
F32 = jnp.float32
BF16 = jnp.bfloat16
ROWS = (((0,), (0,)), ((), ()))
LANES = (((1,), (1,)), ((), ()))
PLAIN = (((1,), (0,)), ((), ()))


def swap(value, axis, offset):
    size = lax.axis_size(axis)
    return lax.ppermute(value, axis, [(i, i ^ offset) for i in range(size)])


def far_first(size):
    return [k for k in range(1, size) if k >= size // 2] + [k for k in range(1, size // 2)]


def pick(value, index, axis):
    return lax.dynamic_index_in_dim(value, index, axis, keepdims=False)


def split(value):
    high = value.astype(BF16)
    return high, (value - high.astype(F32)).astype(BF16)


def dot3(left, right, dims):
    dot = functools.partial(lax.dot_general, dimension_numbers=dims, preferred_element_type=F32)
    return dot(left[0], right[0]) + (dot(left[0], right[1]) + dot(left[1], right[0]))


def whole_spec(shape):
    return pl.BlockSpec(shape, lambda i, s: (0,) * len(shape))


def fy_kernel(ny, nx, s_ref, own_ref, *refs):
    pieces, (high_ref, low_ref, scratch) = refs[:nx], refs[nx:]
    depth = own_ref.shape[0]
    small = depth // nx
    scratch[pl.ds(pl.multiple_of(s_ref[1] * depth, depth), depth), :] = own_ref[...]
    for o in range(nx):
        for k in range(1, ny):
            start = (s_ref[1] ^ k) * depth + (s_ref[0] ^ o) * small
            scratch[pl.ds(pl.multiple_of(start, small), small), :] = pieces[o][k - 1]
    high_ref[...], low_ref[...] = split(scratch[...])


def gather_fy(sizes, where, factor_y, pieces):
    nx, ny = sizes[:2]
    depth, rank = factor_y.shape
    shape = (ny * depth, rank)
    return pl.pallas_call(
        functools.partial(fy_kernel, ny, nx),
        grid_spec=pltpu.PrefetchScalarGridSpec(
            num_scalar_prefetch=1,
            grid=(1,),
            in_specs=[whole_spec(factor_y.shape)] + [whole_spec(p.shape) for p in pieces],
            out_specs=[whole_spec(shape)] * 2,
            scratch_shapes=[pltpu.VMEM(shape, F32)],
        ),
        out_shape=[jax.ShapeDtypeStruct(shape, BF16)] * 2,
        cost_estimate=pl.CostEstimate(flops=1000, bytes_accessed=1 << 20, transcendentals=0),
    )(where, factor_y, *pieces)


def chunk_kernel(sizes, first, last, s_ref, *refs):
    nx, ny, _ = sizes
    fields, refs = refs[:ny], refs[ny:]
    (fyh_ref, fyl_ref, fxt_ref), refs = refs[:3], refs[3:]
    if not first:
        gin_ref, refs = refs[0], refs[1:]
    keep_ref, sent_ref, refs = refs[0], refs[1], refs[2:]
    if last:
        gkeep_ref, gsent_ref, wide_ref, gram_ref = refs
    else:
        gram_ref, wide_ref = refs
    step = pl.program_id(0)
    pair, x_local, y_local = fields[0].shape
    me_x, me_y = s_ref[0], s_ref[1]
    for k in range(ny):
        start = pl.multiple_of((me_y ^ k) * y_local, y_local)
        wide_ref[:, pl.ds(start, y_local)] = fields[k][...].reshape(pair * x_local, y_local)
    wide = split(wide_ref[...])
    gram = dot3(wide, wide, ROWS)

    @pl.when(step == 0)
    def _():
        gram_ref[...] = gram if first else gin_ref[...] + gram

    @pl.when(step > 0)
    def _():
        gram_ref[...] += gram

    half = dot3(wide, (fyh_ref[...], fyl_ref[...]), PLAIN)
    b_block = half.shape[1] // ny
    paired = jnp.concatenate(
        [
            half[p * x_local : (p + 1) * x_local, q * b_block : (q + 1) * b_block]
            for q in range(ny)
            for p in range(pair)
        ],
        axis=1,
    )
    a_block = fxt_ref.shape[0] // nx
    fx = jnp.concatenate(
        [
            fxt_ref[pl.ds(pl.multiple_of((me_x ^ o) * a_block, a_block), a_block), :]
            for o in range(nx)
        ],
        axis=0,
    )
    full = dot3(split(fx), split(paired), PLAIN)
    lanes = pair * b_block
    for o in range(nx):
        target = sent_ref if o % 2 else keep_ref
        for q in range(ny):
            target[o // 2, q, 0] = full[
                o * a_block : (o + 1) * a_block, q * lanes : (q + 1) * lanes
            ]
    if last:

        @pl.when(step == pl.num_programs(0) - 1)
        def _():
            part = y_local // 2
            bit = me_x & 1
            for k in range(ny):
                mine = pl.multiple_of(k * y_local + bit * part, part)
                other = pl.multiple_of(k * y_local + (1 - bit) * part, part)
                gkeep_ref[k] = gram_ref[pl.ds(mine, part), :]
                gsent_ref[k] = gram_ref[pl.ds(other, part), :]


def chunk_terms(sizes, where, flat, offset, parts, fy, fxt, gram, last):
    nx, ny, _ = sizes
    n, x_local, y_local = parts[0].shape
    own = flat.shape[0] // ny
    rank = fxt.shape[0]
    pairs = n // 2
    width = ny * y_local
    a_block, b_block = rank // nx, rank // ny
    half = (nx // 2, ny, pairs, a_block, 2 * b_block)
    field = (2, x_local, y_local)
    specs = [pl.BlockSpec(field, lambda i, s: ((s[1] * own + offset) // 2 + i, 0, 0))]
    specs += [pl.BlockSpec(field, lambda i, s: (i, 0, 0))] * (ny - 1)
    specs += [whole_spec(fy[0].shape)] * 2 + [whole_spec(fxt.shape)]
    args = [flat, *parts, *fy, fxt]
    first = gram is None
    if not first:
        specs.append(whole_spec((width, width)))
        args.append(gram)
    half_spec = pl.BlockSpec(
        (nx // 2, ny, 1, a_block, 2 * b_block), lambda i, s: (0, 0, i, 0, 0)
    )
    out_specs = [half_spec] * 2
    out_shape = [jax.ShapeDtypeStruct(half, F32)] * 2
    scratch = [pltpu.VMEM((2 * x_local, width), F32)]
    if last:
        gshape = (ny, y_local // 2, width)
        out_specs += [whole_spec(gshape)] * 2
        out_shape += [jax.ShapeDtypeStruct(gshape, F32)] * 2
        scratch.append(pltpu.VMEM((width, width), F32))
    else:
        out_specs.append(whole_spec((width, width)))
        out_shape.append(jax.ShapeDtypeStruct((width, width), F32))
    flops = 2 * n * x_local * (width * width + width * rank + rank * rank) * 3
    return pl.pallas_call(
        functools.partial(chunk_kernel, sizes, first, last),
        grid_spec=pltpu.PrefetchScalarGridSpec(
            num_scalar_prefetch=1,
            grid=(pairs,),
            in_specs=specs,
            out_specs=out_specs,
            scratch_shapes=scratch,
        ),
        out_shape=out_shape,
        cost_estimate=pl.CostEstimate(flops=flops, bytes_accessed=1 << 22, transcendentals=0),
    )(where, *args)


def gram_x_kernel(sizes, s_ref, *refs):
    nx = sizes[0]
    fields, (keep_ref, sent_ref, tall_ref, gram_ref) = refs[:nx], refs[nx:]
    pair, x_local, y_local = fields[0].shape
    me_x = s_ref[0]
    for o in range(nx):
        start = pl.multiple_of((me_x ^ o) * x_local, x_local)
        for p in range(pair):
            tall_ref[pl.ds(start, x_local), p * y_local : (p + 1) * y_local] = fields[o][p]
    tall = split(tall_ref[...])
    gram = dot3(tall, tall, LANES)
    step = pl.program_id(0)

    @pl.when(step == 0)
    def _():
        gram_ref[...] = gram

    @pl.when(step > 0)
    def _():
        gram_ref[...] += gram

    @pl.when(step == pl.num_programs(0) - 1)
    def _():
        bit = me_x & 1
        for j in range(nx // 2):
            mine = pl.multiple_of((2 * j + bit) * x_local, x_local)
            other = pl.multiple_of((2 * j + 1 - bit) * x_local, x_local)
            keep_ref[j] = gram_ref[pl.ds(mine, x_local), :]
            sent_ref[j] = gram_ref[pl.ds(other, x_local), :]


def gram_x_terms(sizes, where, flat, parts):
    nx = sizes[0]
    own, x_local, y_local = parts[0].shape
    width = nx * x_local
    field = (2, x_local, y_local)
    specs = [pl.BlockSpec(field, lambda i, s: (s[0] * own // 2 + i, 0, 0))]
    specs += [pl.BlockSpec(field, lambda i, s: (i, 0, 0))] * (nx - 1)
    half = (nx // 2, x_local, width)
    flops = 2 * own * y_local * width * width * 3
    return pl.pallas_call(
        functools.partial(gram_x_kernel, sizes),
        grid_spec=pltpu.PrefetchScalarGridSpec(
            num_scalar_prefetch=1,
            grid=(own // 2,),
            in_specs=specs,
            out_specs=[whole_spec(half)] * 2,
            scratch_shapes=[pltpu.VMEM((width, 2 * y_local), F32), pltpu.VMEM((width, width), F32)],
        ),
        out_shape=[jax.ShapeDtypeStruct(half, F32)] * 2,
        cost_estimate=pl.CostEstimate(flops=flops, bytes_accessed=1 << 23, transcendentals=0),
    )(where, flat, *parts)


def unpack_kernel(ny, n, own, s_ref, *refs):
    parts, out_ref = refs[:-1], refs[-1]
    chunks = len(parts) // ny
    b_block = out_ref.shape[2]
    for k in range(ny):
        for c in range(chunks):
            part = parts[c * ny + k]
            for j in range(n // 2):
                base = (s_ref[1] ^ k) * own + c * n + 2 * j
                out_ref[base] = part[j, :, :b_block]
                out_ref[base + 1] = part[j, :, b_block:]


def unpack(sizes, where, parts, rows):
    ny = sizes[1]
    half, a_block, lanes = parts[0].shape
    shape = (rows, a_block, lanes // 2)
    return pl.pallas_call(
        functools.partial(unpack_kernel, ny, 2 * half, rows // ny),
        grid_spec=pltpu.PrefetchScalarGridSpec(
            num_scalar_prefetch=1,
            grid=(1,),
            in_specs=[whole_spec(p.shape) for p in parts],
            out_specs=whole_spec(shape),
        ),
        out_shape=jax.ShapeDtypeStruct(shape, F32),
        cost_estimate=pl.CostEstimate(flops=1000, bytes_accessed=3 << 20, transcendentals=0),
    )(where, *parts)


def local_step(slab, factor_x, factor_y):
    z_cells, s_local, x_local, y_local = slab.shape
    sizes = nx, ny, ns = tuple(lax.axis_size(a) for a in ("gx", "gy", "sa"))
    me_x, me_y, me_s = (lax.axis_index(a) for a in ("gx", "gy", "sa"))
    where = jnp.stack([me_x, me_y, me_s]).astype(jnp.int32)
    rank = factor_x.shape[1]
    a_block, b_block = rank // nx, rank // ny
    rows = z_cells * s_local
    flat = slab.reshape((rows, x_local, y_local))
    own_y, own_x = rows // ny, rows // nx
    n = own_y // CHUNKS
    x_total, y_total, s_total = x_local * nx, y_local * ny, s_local * ns

    source = flat
    along_y = []
    for c in range(CHUNKS):
        cut = {
            k: lax.dynamic_slice_in_dim(source, (me_y ^ k) * own_y + c * n, n, 0)
            for k in far_first(ny)
        }
        source, cut = lax.optimization_barrier((source, cut))
        along_y.append({k: swap(cut[k], "gy", k) for k in far_first(ny)})
        if c == 0:
            mine = pick(factor_y.reshape((nx, y_local // nx, rank)), me_x, 0)
            crossed = jnp.stack([swap(mine, "gy", k) for k in range(1, ny)])
            pieces = [crossed] + [swap(crossed, "gx", o) for o in range(1, nx)]
            cut = {
                k: lax.dynamic_slice_in_dim(source, (me_x ^ k) * own_x, own_x, 0)
                for k in far_first(nx)
            }
            source, cut = lax.optimization_barrier((source, cut))
            along_x = {k: swap(cut[k], "gx", k) for k in far_first(nx)}
    fy = gather_fy(sizes, where, factor_y, pieces)
    fxt = factor_x.T

    gram = None
    core_parts = []
    for c in range(CHUNKS):
        parts = [along_y[c][k] for k in range(1, ny)]
        last = c == CHUNKS - 1
        out = chunk_terms(sizes, where, flat, c * n, parts, fy, fxt, gram, last)
        keep, sent, gram = out[0], out[1], out[2:]
        if last:
            gkeep, gsent = gram
            ggot = swap(gsent, "gx", 1)
        else:
            gram = gram[0]
        bit = 1
        while bit < nx:
            got = swap(sent, "gx", bit)
            keep = keep + got
            if 2 * bit < nx:
                sent = keep[1::2]
                keep = keep[0::2]
            bit *= 2
        keep = keep[0]
        z_parts = [pick(keep, me_y ^ k, 0) for k in range(ny)]
        core_parts += [swap(z_parts[k], "gy", k) if k else z_parts[0] for k in range(ny)]
    core = unpack(sizes, where, core_parts, rows)
    core = core.reshape((z_cells, s_local, a_block, b_block))

    keep, sent = gram_x_terms(sizes, where, flat, [along_x[k] for k in range(1, nx)])
    got = swap(sent, "gx", 1)
    bit = 2
    while bit < nx:
        keep = keep.reshape((-1, 2, x_local, x_total))
        got = got.reshape((-1, 2, x_local, x_total))
        mybit = (me_x // bit) & 1
        sent = pick(keep, 1 - mybit, 1) + pick(got, 1 - mybit, 1)
        keep = pick(keep, mybit, 1) + pick(got, mybit, 1)
        got = swap(sent, "gx", bit)
        bit *= 2
    total = (keep[0] + got[0]).reshape((ny, ns, -1, x_total))
    keep = pick(total, me_s, 1)
    for k in range(1, ns):
        keep = keep + swap(pick(total, me_s ^ k, 1), "sa", k)
    gram_x = pick(keep, me_y, 0)
    for k in range(1, ny):
        gram_x = gram_x + swap(pick(keep, me_y ^ k, 0), "gy", k)
    gram_x = gram_x / (y_total * z_cells * s_total)

    keep, got = gkeep, ggot
    bit = 2
    while bit < nx:
        shape = (ny, 2, keep.shape[1] // 2, y_total)
        keep, got = keep.reshape(shape), got.reshape(shape)
        mybit = (me_x // bit) & 1
        sent = pick(keep, 1 - mybit, 1) + pick(got, 1 - mybit, 1)
        keep = pick(keep, mybit, 1) + pick(got, mybit, 1)
        got = swap(sent, "gx", bit)
        bit *= 2
    total = (keep + got).reshape((ny, ns, -1, y_total))
    keep = pick(total, me_s, 1)
    for k in range(1, ns):
        keep = keep + swap(pick(total, me_s ^ k, 1), "sa", k)
    row = pick(keep, me_y, 0)
    for k in range(1, ny):
        row = row + swap(pick(keep, me_y ^ k, 0), "gy", k)
    row = row / (x_total * z_cells * s_total)
    both = jnp.stack([row] + [swap(row, "sa", k) for k in range(1, ns)])
    cur = jnp.concatenate([pick(both, me_s ^ k, 0) for k in range(ns)], axis=0)
    bit = nx // 2
    while bit:
        got = swap(cur, "gx", bit)
        high = (me_x // bit) % 2 == 1
        cur = jnp.concatenate([jnp.where(high, got, cur), jnp.where(high, cur, got)], axis=0)
        bit //= 2
    return (gram_x, cur, core)


def solution(mesh):
    in_specs = (P(None, "sa", "gx", "gy"), P("gx", None), P("gy", None))
    out_specs = (P(("gx", "gy", "sa"), None), P("gy", None), P(None, "sa", "gx", "gy"))
    return jax.shard_map(
        local_step, mesh=mesh, in_specs=in_specs, out_specs=out_specs, check_vma=False
    )
```

```python
import functools

import jax
import jax.numpy as jnp
from jax import lax
from jax.experimental import pallas as pl
from jax.experimental.pallas import tpu as pltpu
from jax.sharding import PartitionSpec as P


F32 = jnp.float32
BF16 = jnp.bfloat16
ROWS = (((0,), (0,)), ((), ()))
LANES = (((1,), (1,)), ((), ()))
PLAIN = (((1,), (0,)), ((), ()))


def swap(value, axis, offset):
    size = lax.axis_size(axis)
    return lax.ppermute(value, axis, [(i, i ^ offset) for i in range(size)])


def pick(value, index, axis):
    return lax.dynamic_index_in_dim(value, index, axis, keepdims=False)


def split(value):
    high = value.astype(BF16)
    return high, (value - high.astype(F32)).astype(BF16)


def dot3(left, right, dims):
    (lc,), (rc,) = dims[0]
    lhs = jnp.concatenate([left[0], left[0], left[1]], axis=lc)
    rhs = jnp.concatenate([right[0], right[1], right[0]], axis=rc)
    return lax.dot_general(lhs, rhs, dims, preferred_element_type=F32)


def params():
    return pltpu.CompilerParams(vmem_limit_bytes=24 << 20)


def chunk_sizes(own):
    edge = max(2, own // 8)
    middle = (own - 2 * edge) // 2
    sizes = (edge, middle, own - 2 * edge - middle, edge)
    assert all(n > 0 and n % 2 == 0 for n in sizes)
    return sizes


def whole_spec(shape):
    return pl.BlockSpec(shape, lambda i, s: (0,) * len(shape))


def cut_kernel(s_ref, *refs):
    half = len(refs) // 2
    for source, target in zip(refs[:half], refs[half:]):
        target[...] = source[...]


def cut(where, flat, pieces):
    block = (2,) + flat.shape[1:]
    steps = max(size for *_, size in pieces) // 2
    in_specs, out_specs, out_shape = [], [], []
    for axis, k, own, start, size in pieces:

        def source(i, s, axis=axis, k=k, own=own, start=start, size=size):
            return (((s[axis] ^ k) * own + start) // 2 + jnp.minimum(i, size // 2 - 1), 0, 0)

        def target(i, s, size=size):
            return (jnp.minimum(i, size // 2 - 1), 0, 0)

        in_specs.append(pl.BlockSpec(block, source))
        out_specs.append(pl.BlockSpec(block, target))
        out_shape.append(jax.ShapeDtypeStruct((size,) + flat.shape[1:], F32))
    return pl.pallas_call(
        cut_kernel,
        grid_spec=pltpu.PrefetchScalarGridSpec(
            num_scalar_prefetch=1, grid=(steps,), in_specs=in_specs, out_specs=out_specs
        ),
        out_shape=out_shape,
        compiler_params=params(),
        cost_estimate=pl.CostEstimate(flops=1000, bytes_accessed=1 << 22, transcendentals=0),
    )(where, *[flat] * len(pieces))


def reverse_bits(value, count):
    bits = count.bit_length() - 1
    return sum(((value >> i) & 1) << (bits - 1 - i) for i in range(bits))


def rows_kernel(terms, s_ref, *refs):
    parts, out_ref = refs[:-1], refs[-1]
    size = parts[0].shape[0]
    for o, part in enumerate(parts):
        place = reverse_bits(s_ref[0] ^ o, len(parts))
        out_ref[pl.ds(pl.multiple_of(place * size, size), size), :] = part[...] / terms


def place_rows(where, parts, terms):
    size, width = parts[0].shape
    shape = (len(parts) * size, width)
    return pl.pallas_call(
        functools.partial(rows_kernel, terms),
        grid_spec=pltpu.PrefetchScalarGridSpec(
            num_scalar_prefetch=1,
            grid=(1,),
            in_specs=[whole_spec((size, width))] * len(parts),
            out_specs=whole_spec(shape),
        ),
        out_shape=jax.ShapeDtypeStruct(shape, F32),
        compiler_params=params(),
        cost_estimate=pl.CostEstimate(flops=1000, bytes_accessed=1 << 19, transcendentals=0),
    )(where, *parts)


def fy_kernel(ny, nx, s_ref, own_ref, *refs):
    pieces, (high_ref, low_ref, scratch) = refs[:nx], refs[nx:]
    depth = own_ref.shape[0]
    small = depth // nx
    scratch[pl.ds(pl.multiple_of(s_ref[1] * depth, depth), depth), :] = own_ref[...]
    for o in range(nx):
        for k in range(1, ny):
            start = (s_ref[1] ^ k) * depth + (s_ref[0] ^ o) * small
            scratch[pl.ds(pl.multiple_of(start, small), small), :] = pieces[o][k - 1]
    high_ref[...], low_ref[...] = split(scratch[...])


def gather_fy(sizes, where, factor_y, pieces):
    nx, ny = sizes[:2]
    depth, rank = factor_y.shape
    shape = (ny * depth, rank)
    return pl.pallas_call(
        functools.partial(fy_kernel, ny, nx),
        grid_spec=pltpu.PrefetchScalarGridSpec(
            num_scalar_prefetch=1,
            grid=(1,),
            in_specs=[whole_spec(factor_y.shape)] + [whole_spec(p.shape) for p in pieces],
            out_specs=[whole_spec(shape)] * 2,
            scratch_shapes=[pltpu.VMEM(shape, F32)],
        ),
        out_shape=[jax.ShapeDtypeStruct(shape, BF16)] * 2,
        compiler_params=params(),
        cost_estimate=pl.CostEstimate(flops=1000, bytes_accessed=1 << 20, transcendentals=0),
    )(where, factor_y, *pieces)


def chunk_kernel(sizes, first, last, s_ref, *refs):
    nx, ny, _ = sizes
    fields, refs = refs[:ny], refs[ny:]
    (fyh_ref, fyl_ref, fxt_ref), refs = refs[:3], refs[3:]
    if not first:
        gin_ref, refs = refs[0], refs[1:]
    keep_ref, sent_ref, refs = refs[0], refs[1], refs[2:]
    if last:
        gkeep_ref, gsent_ref, wide_ref, gram_ref = refs
    else:
        gram_ref, wide_ref = refs
    n, x_local, y_local = fields[0].shape
    me_x, me_y = s_ref[0], s_ref[1]
    for k in range(ny):
        start = pl.multiple_of((me_y ^ k) * y_local, y_local)
        wide_ref[:, pl.ds(start, y_local)] = fields[k][...].reshape(n * x_local, y_local)
    wide = split(wide_ref[...])
    gram = dot3(wide, wide, ROWS)
    gram_ref[...] = gram if first else gin_ref[...] + gram

    half = dot3(wide, (fyh_ref[...], fyl_ref[...]), PLAIN)
    b_block = half.shape[1] // ny
    paired = jnp.concatenate(
        [
            half[p * x_local : (p + 1) * x_local, q * b_block : (q + 1) * b_block]
            for j in range(n // 2)
            for q in range(ny)
            for p in (2 * j, 2 * j + 1)
        ],
        axis=1,
    )
    a_block = fxt_ref.shape[0] // nx
    fx = jnp.concatenate(
        [
            fxt_ref[pl.ds(pl.multiple_of((me_x ^ o) * a_block, a_block), a_block), :]
            for o in range(nx)
        ],
        axis=0,
    )
    full = dot3(split(fx), split(paired), PLAIN)
    lanes = 2 * b_block
    for o in range(nx):
        target = sent_ref if o % 2 else keep_ref
        for j in range(n // 2):
            for q in range(ny):
                at = (j * ny + q) * lanes
                target[o // 2, q, j] = full[o * a_block : (o + 1) * a_block, at : at + lanes]
    if last:
        part = y_local // 2
        bit = me_x & 1
        for k in range(ny):
            mine = pl.multiple_of(k * y_local + bit * part, part)
            other = pl.multiple_of(k * y_local + (1 - bit) * part, part)
            gkeep_ref[k] = gram_ref[pl.ds(mine, part), :]
            gsent_ref[k] = gram_ref[pl.ds(other, part), :]


def chunk_terms(sizes, where, parts, fy, fxt, gram, last):
    nx, ny, _ = sizes
    n, x_local, y_local = parts[0].shape
    rank = fxt.shape[0]
    pairs = n // 2
    width = ny * y_local
    a_block, b_block = rank // nx, rank // ny
    half = (nx // 2, ny, pairs, a_block, 2 * b_block)
    field = (n, x_local, y_local)
    specs = [whole_spec(field)] * ny
    specs += [whole_spec(fy[0].shape)] * 2 + [whole_spec(fxt.shape)]
    args = [*parts, *fy, fxt]
    first = gram is None
    if not first:
        specs.append(whole_spec((width, width)))
        args.append(gram)
    out_specs = [whole_spec(half)] * 2
    out_shape = [jax.ShapeDtypeStruct(half, F32)] * 2
    scratch = [pltpu.VMEM((n * x_local, width), F32)]
    if last:
        gshape = (ny, y_local // 2, width)
        out_specs += [whole_spec(gshape)] * 2
        out_shape += [jax.ShapeDtypeStruct(gshape, F32)] * 2
        scratch.append(pltpu.VMEM((width, width), F32))
    else:
        out_specs.append(whole_spec((width, width)))
        out_shape.append(jax.ShapeDtypeStruct((width, width), F32))
    flops = 2 * n * x_local * (width * width + width * rank + rank * rank) * 3
    return pl.pallas_call(
        functools.partial(chunk_kernel, sizes, first, last),
        grid_spec=pltpu.PrefetchScalarGridSpec(
            num_scalar_prefetch=1,
            grid=(1,),
            in_specs=specs,
            out_specs=out_specs,
            scratch_shapes=scratch,
        ),
        out_shape=out_shape,
        compiler_params=params(),
        cost_estimate=pl.CostEstimate(flops=flops, bytes_accessed=1 << 22, transcendentals=0),
    )(where, *args)


def gram_x_kernel(sizes, s_ref, *refs):
    nx = sizes[0]
    fields, (keep_ref, sent_ref, tall_ref, gram_ref) = refs[:nx], refs[nx:]
    pair, x_local, y_local = fields[0].shape
    me_x = s_ref[0]
    for o in range(nx):
        start = pl.multiple_of((me_x ^ o) * x_local, x_local)
        for p in range(pair):
            tall_ref[pl.ds(start, x_local), p * y_local : (p + 1) * y_local] = fields[o][p]
    tall = split(tall_ref[...])
    gram = dot3(tall, tall, LANES)
    step = pl.program_id(0)

    @pl.when(step == 0)
    def _():
        gram_ref[...] = gram

    @pl.when(step > 0)
    def _():
        gram_ref[...] += gram

    @pl.when(step == pl.num_programs(0) - 1)
    def _():
        bit = me_x & 1
        for j in range(nx // 2):
            mine = pl.multiple_of((2 * j + bit) * x_local, x_local)
            other = pl.multiple_of((2 * j + 1 - bit) * x_local, x_local)
            keep_ref[j] = gram_ref[pl.ds(mine, x_local), :]
            sent_ref[j] = gram_ref[pl.ds(other, x_local), :]


def gram_x_terms(sizes, where, flat, parts):
    nx = sizes[0]
    own, x_local, y_local = parts[0].shape
    width = nx * x_local
    batch = 4
    field = (batch, x_local, y_local)
    specs = [pl.BlockSpec(field, lambda i, s: (s[0] * own // batch + i, 0, 0))]
    specs += [pl.BlockSpec(field, lambda i, s: (i, 0, 0))] * (nx - 1)
    half = (nx // 2, x_local, width)
    flops = 2 * own * y_local * width * width * 3
    return pl.pallas_call(
        functools.partial(gram_x_kernel, sizes),
        grid_spec=pltpu.PrefetchScalarGridSpec(
            num_scalar_prefetch=1,
            grid=(own // batch,),
            in_specs=specs,
            out_specs=[whole_spec(half)] * 2,
            scratch_shapes=[pltpu.VMEM((width, batch * y_local), F32), pltpu.VMEM((width, width), F32)],
        ),
        out_shape=[jax.ShapeDtypeStruct(half, F32)] * 2,
        compiler_params=params(),
        cost_estimate=pl.CostEstimate(flops=flops, bytes_accessed=1 << 23, transcendentals=0),
    )(where, flat, *parts)


def unpack_kernel(ny, own, starts, s_ref, *refs):
    parts, out_ref = refs[:-1], refs[-1]
    b_block = out_ref.shape[2]
    for c, start in enumerate(starts):
        for k in range(ny):
            part = parts[c * ny + k]
            for j in range(part.shape[0]):
                base = (s_ref[1] ^ k) * own + start + 2 * j
                out_ref[base] = part[j, :, :b_block]
                out_ref[base + 1] = part[j, :, b_block:]


def unpack(sizes, where, parts, starts, rows):
    ny = sizes[1]
    _, a_block, lanes = parts[0].shape
    shape = (rows, a_block, lanes // 2)
    return pl.pallas_call(
        functools.partial(unpack_kernel, ny, rows // ny, starts),
        grid_spec=pltpu.PrefetchScalarGridSpec(
            num_scalar_prefetch=1,
            grid=(1,),
            in_specs=[whole_spec(p.shape) for p in parts],
            out_specs=whole_spec(shape),
        ),
        out_shape=jax.ShapeDtypeStruct(shape, F32),
        compiler_params=params(),
        cost_estimate=pl.CostEstimate(flops=1000, bytes_accessed=3 << 20, transcendentals=0),
    )(where, *parts)


def local_step(slab, factor_x, factor_y):
    z_cells, s_local, x_local, y_local = slab.shape
    sizes = nx, ny, ns = tuple(lax.axis_size(a) for a in ("gx", "gy", "sa"))
    me_x, me_y, me_s = (lax.axis_index(a) for a in ("gx", "gy", "sa"))
    where = jnp.stack([me_x, me_y, me_s]).astype(jnp.int32)
    rank = factor_x.shape[1]
    a_block, b_block = rank // nx, rank // ny
    rows = z_cells * s_local
    flat = slab.reshape((rows, x_local, y_local))
    own_y, own_x = rows // ny, rows // nx
    counts = chunk_sizes(own_y)
    starts = [sum(counts[:c]) for c in range(len(counts))]
    x_total, y_total, s_total = x_local * nx, y_local * ny, s_local * ns

    keys = [[(1, k, own_y, starts[c], counts[c]) for k in range(ny)] for c in range(len(counts))]
    x_keys = [(0, k, own_x, 0, own_x) for k in range(1, nx)]
    groups = [keys[0][1:], x_keys, [keys[0][0]] + sum(keys[1:], [])]
    pieces = {}
    for group in groups:
        pieces.update(zip(group, cut(where, flat, group)))
    along_y = []
    for c in range(len(counts)):
        here = [pieces[keys[c][0]]]
        here += [swap(pieces[keys[c][k]], "gy", k) for k in range(1, ny)]
        along_y.append(here)
    along_x = [swap(pieces[x_keys[k - 1]], "gx", k) for k in range(1, nx)]
    mine = pick(factor_y.reshape((nx, y_local // nx, rank)), me_x, 0)
    crossed = jnp.stack([swap(mine, "gy", k) for k in range(1, ny)])
    fy_parts = [crossed] + [swap(crossed, "gx", o) for o in range(1, nx)]
    fy = gather_fy(sizes, where, factor_y, fy_parts)
    fxt = factor_x.T

    gram = None
    core_parts = []
    for c in range(len(counts)):
        last = c == len(counts) - 1
        out = chunk_terms(sizes, where, along_y[c], fy, fxt, gram, last)
        keep, sent, gram = out[0], out[1], out[2:]
        if last:
            gkeep, gsent = gram
            ggot = swap(gsent, "gx", 1)
        else:
            gram = gram[0]
        bit = 1
        while bit < nx:
            got = swap(sent, "gx", bit)
            keep = keep + got
            if 2 * bit < nx:
                sent = keep[1::2]
                keep = keep[0::2]
            bit *= 2
        keep = keep[0]
        z_parts = [pick(keep, me_y ^ k, 0) for k in range(ny)]
        core_parts += [swap(z_parts[k], "gy", k) if k else z_parts[0] for k in range(ny)]
    core = unpack(sizes, where, core_parts, starts, rows)
    core = core.reshape((z_cells, s_local, a_block, b_block))

    keep, sent = gram_x_terms(sizes, where, flat, along_x)
    got = swap(sent, "gx", 1)
    bit = 2
    while bit < nx:
        keep = keep.reshape((-1, 2, x_local, x_total))
        got = got.reshape((-1, 2, x_local, x_total))
        mybit = (me_x // bit) & 1
        sent = pick(keep, 1 - mybit, 1) + pick(got, 1 - mybit, 1)
        keep = pick(keep, mybit, 1) + pick(got, mybit, 1)
        got = swap(sent, "gx", bit)
        bit *= 2
    total = (keep[0] + got[0]).reshape((ny, ns, -1, x_total))
    keep = pick(total, me_s, 1)
    for k in range(1, ns):
        keep = keep + swap(pick(total, me_s ^ k, 1), "sa", k)
    gram_x = pick(keep, me_y, 0)
    for k in range(1, ny):
        gram_x = gram_x + swap(pick(keep, me_y ^ k, 0), "gy", k)
    gram_x = gram_x / (y_total * z_cells * s_total)

    keep, got = gkeep, ggot
    bit = 2
    while bit < nx:
        shape = (ny, 2, keep.shape[1] // 2, y_total)
        keep, got = keep.reshape(shape), got.reshape(shape)
        mybit = (me_x // bit) & 1
        sent = pick(keep, 1 - mybit, 1) + pick(got, 1 - mybit, 1)
        keep = pick(keep, mybit, 1) + pick(got, mybit, 1)
        got = swap(sent, "gx", bit)
        bit *= 2
    total = keep + got
    row = pick(total, me_y, 0)
    for k in range(1, ny):
        row = row + swap(pick(total, me_y ^ k, 0), "gy", k)
    summed = row
    for k in range(1, ns):
        summed = summed + swap(row, "sa", k)
    parts = [summed] + [swap(summed, "gx", o) for o in range(1, nx)]
    gram_y = place_rows(where, parts, x_total * z_cells * s_total)
    return (gram_x, gram_y, core)


def solution(mesh):
    in_specs = (P(None, "sa", "gx", "gy"), P("gx", None), P("gy", None))
    out_specs = (P(("gx", "gy", "sa"), None), P("gy", None), P(None, "sa", "gx", "gy"))
    return jax.shard_map(
        local_step, mesh=mesh, in_specs=in_specs, out_specs=out_specs, check_vma=False
    )
```

```python
import functools

import jax
import jax.numpy as jnp
from jax import lax
from jax.experimental import pallas as pl
from jax.experimental.pallas import tpu as pltpu
from jax.sharding import PartitionSpec as P


F32 = jnp.float32
BF16 = jnp.bfloat16
ROWS = (((0,), (0,)), ((), ()))
LANES = (((1,), (1,)), ((), ()))
PLAIN = (((1,), (0,)), ((), ()))


def swap(value, axis, offset):
    size = lax.axis_size(axis)
    return lax.ppermute(value, axis, [(i, i ^ offset) for i in range(size)])


def pick(value, index, axis):
    return lax.dynamic_index_in_dim(value, index, axis, keepdims=False)


def split(value):
    high = value.astype(BF16)
    return high, (value - high.astype(F32)).astype(BF16)


def dot3(left, right, dims):
    (lc,), (rc,) = dims[0]
    lhs = jnp.concatenate([left[0], left[0], left[1]], axis=lc)
    rhs = jnp.concatenate([right[0], right[1], right[0]], axis=rc)
    return lax.dot_general(lhs, rhs, dims, preferred_element_type=F32)


def params():
    return pltpu.CompilerParams(vmem_limit_bytes=24 << 20)


def chunk_sizes(own):
    sizes = (own // 2, own // 2 - max(2, own // 8), max(2, own // 8))
    assert all(n > 0 and n % 2 == 0 for n in sizes)
    return sizes


def whole_spec(shape):
    return pl.BlockSpec(shape, lambda i, s: (0,) * len(shape))


def cut_kernel(s_ref, *refs):
    half = len(refs) // 2
    for source, target in zip(refs[:half], refs[half:]):
        target[...] = source[...]


def cut(where, flat, pieces):
    block = (2,) + flat.shape[1:]
    steps = max(size for *_, size in pieces) // 2
    in_specs, out_specs, out_shape = [], [], []
    for axis, k, own, start, size in pieces:

        def source(i, s, axis=axis, k=k, own=own, start=start, size=size):
            return (((s[axis] ^ k) * own + start) // 2 + jnp.minimum(i, size // 2 - 1), 0, 0)

        def target(i, s, size=size):
            return (jnp.minimum(i, size // 2 - 1), 0, 0)

        in_specs.append(pl.BlockSpec(block, source))
        out_specs.append(pl.BlockSpec(block, target))
        out_shape.append(jax.ShapeDtypeStruct((size,) + flat.shape[1:], F32))
    return pl.pallas_call(
        cut_kernel,
        grid_spec=pltpu.PrefetchScalarGridSpec(
            num_scalar_prefetch=1, grid=(steps,), in_specs=in_specs, out_specs=out_specs
        ),
        out_shape=out_shape,
        cost_estimate=pl.CostEstimate(flops=1000, bytes_accessed=1 << 22, transcendentals=0),
    )(where, *[flat] * len(pieces))


def reverse_bits(value, count):
    bits = count.bit_length() - 1
    return sum(((value >> i) & 1) << (bits - 1 - i) for i in range(bits))


def rows_kernel(terms, s_ref, *refs):
    parts, out_ref = refs[:-1], refs[-1]
    size = parts[0].shape[0]
    for o, part in enumerate(parts):
        place = reverse_bits(s_ref[0] ^ o, len(parts))
        out_ref[pl.ds(pl.multiple_of(place * size, size), size), :] = part[...] / terms


def place_rows(where, parts, terms):
    size, width = parts[0].shape
    shape = (len(parts) * size, width)
    return pl.pallas_call(
        functools.partial(rows_kernel, terms),
        grid_spec=pltpu.PrefetchScalarGridSpec(
            num_scalar_prefetch=1,
            grid=(1,),
            in_specs=[whole_spec((size, width))] * len(parts),
            out_specs=whole_spec(shape),
        ),
        out_shape=jax.ShapeDtypeStruct(shape, F32),
        compiler_params=params(),
        cost_estimate=pl.CostEstimate(flops=1000, bytes_accessed=1 << 19, transcendentals=0),
    )(where, *parts)


def fy_kernel(ny, nx, s_ref, own_ref, *refs):
    pieces, (high_ref, low_ref, scratch) = refs[:nx], refs[nx:]
    depth = own_ref.shape[0]
    small = depth // nx
    scratch[pl.ds(pl.multiple_of(s_ref[1] * depth, depth), depth), :] = own_ref[...]
    for o in range(nx):
        for k in range(1, ny):
            start = (s_ref[1] ^ k) * depth + (s_ref[0] ^ o) * small
            scratch[pl.ds(pl.multiple_of(start, small), small), :] = pieces[o][k - 1]
    high_ref[...], low_ref[...] = split(scratch[...])


def gather_fy(sizes, where, factor_y, pieces):
    nx, ny = sizes[:2]
    depth, rank = factor_y.shape
    shape = (ny * depth, rank)
    return pl.pallas_call(
        functools.partial(fy_kernel, ny, nx),
        grid_spec=pltpu.PrefetchScalarGridSpec(
            num_scalar_prefetch=1,
            grid=(1,),
            in_specs=[whole_spec(factor_y.shape)] + [whole_spec(p.shape) for p in pieces],
            out_specs=[whole_spec(shape)] * 2,
            scratch_shapes=[pltpu.VMEM(shape, F32)],
        ),
        out_shape=[jax.ShapeDtypeStruct(shape, BF16)] * 2,
        compiler_params=params(),
        cost_estimate=pl.CostEstimate(flops=1000, bytes_accessed=1 << 20, transcendentals=0),
    )(where, factor_y, *pieces)


def chunk_kernel(sizes, first, last, s_ref, *refs):
    nx, ny, _ = sizes
    fields, refs = refs[:ny], refs[ny:]
    (fyh_ref, fyl_ref, fxt_ref), refs = refs[:3], refs[3:]
    if not first:
        gin_ref, refs = refs[0], refs[1:]
    keep_ref, sent_ref, refs = refs[0], refs[1], refs[2:]
    if last:
        gkeep_ref, gsent_ref, wide_ref, gram_ref = refs
    else:
        gram_ref, wide_ref = refs
    n, x_local, y_local = fields[0].shape
    me_x, me_y = s_ref[0], s_ref[1]
    for k in range(ny):
        start = pl.multiple_of((me_y ^ k) * y_local, y_local)
        wide_ref[:, pl.ds(start, y_local)] = fields[k][...].reshape(n * x_local, y_local)
    wide = split(wide_ref[...])
    gram = dot3(wide, wide, ROWS)
    gram_ref[...] = gram if first else gin_ref[...] + gram

    half = dot3(wide, (fyh_ref[...], fyl_ref[...]), PLAIN)
    b_block = half.shape[1] // ny
    paired = jnp.concatenate(
        [
            half[p * x_local : (p + 1) * x_local, q * b_block : (q + 1) * b_block]
            for j in range(n // 2)
            for q in range(ny)
            for p in (2 * j, 2 * j + 1)
        ],
        axis=1,
    )
    a_block = fxt_ref.shape[0] // nx
    fx = jnp.concatenate(
        [
            fxt_ref[pl.ds(pl.multiple_of((me_x ^ o) * a_block, a_block), a_block), :]
            for o in range(nx)
        ],
        axis=0,
    )
    full = dot3(split(fx), split(paired), PLAIN)
    lanes = 2 * b_block
    for o in range(nx):
        target = sent_ref if o % 2 else keep_ref
        for j in range(n // 2):
            for q in range(ny):
                at = (j * ny + q) * lanes
                target[o // 2, q, j] = full[o * a_block : (o + 1) * a_block, at : at + lanes]
    if last:
        part = y_local // 2
        bit = me_x & 1
        for k in range(ny):
            mine = pl.multiple_of(k * y_local + bit * part, part)
            other = pl.multiple_of(k * y_local + (1 - bit) * part, part)
            gkeep_ref[k] = gram_ref[pl.ds(mine, part), :]
            gsent_ref[k] = gram_ref[pl.ds(other, part), :]


def chunk_terms(sizes, where, parts, fy, fxt, gram, last):
    nx, ny, _ = sizes
    n, x_local, y_local = parts[0].shape
    rank = fxt.shape[0]
    pairs = n // 2
    width = ny * y_local
    a_block, b_block = rank // nx, rank // ny
    half = (nx // 2, ny, pairs, a_block, 2 * b_block)
    field = (n, x_local, y_local)
    specs = [whole_spec(field)] * ny
    specs += [whole_spec(fy[0].shape)] * 2 + [whole_spec(fxt.shape)]
    args = [*parts, *fy, fxt]
    first = gram is None
    if not first:
        specs.append(whole_spec((width, width)))
        args.append(gram)
    out_specs = [whole_spec(half)] * 2
    out_shape = [jax.ShapeDtypeStruct(half, F32)] * 2
    scratch = [pltpu.VMEM((n * x_local, width), F32)]
    if last:
        gshape = (ny, y_local // 2, width)
        out_specs += [whole_spec(gshape)] * 2
        out_shape += [jax.ShapeDtypeStruct(gshape, F32)] * 2
        scratch.append(pltpu.VMEM((width, width), F32))
    else:
        out_specs.append(whole_spec((width, width)))
        out_shape.append(jax.ShapeDtypeStruct((width, width), F32))
    flops = 2 * n * x_local * (width * width + width * rank + rank * rank) * 3
    return pl.pallas_call(
        functools.partial(chunk_kernel, sizes, first, last),
        grid_spec=pltpu.PrefetchScalarGridSpec(
            num_scalar_prefetch=1,
            grid=(1,),
            in_specs=specs,
            out_specs=out_specs,
            scratch_shapes=scratch,
        ),
        out_shape=out_shape,
        compiler_params=params(),
        cost_estimate=pl.CostEstimate(flops=flops, bytes_accessed=1 << 22, transcendentals=0),
    )(where, *args)


def gram_x_kernel(sizes, s_ref, *refs):
    nx = sizes[0]
    fields, (keep_ref, sent_ref, tall_ref, gram_ref) = refs[:nx], refs[nx:]
    pair, x_local, y_local = fields[0].shape
    me_x = s_ref[0]
    for o in range(nx):
        start = pl.multiple_of((me_x ^ o) * x_local, x_local)
        for p in range(pair):
            tall_ref[pl.ds(start, x_local), p * y_local : (p + 1) * y_local] = fields[o][p]
    tall = split(tall_ref[...])
    gram = dot3(tall, tall, LANES)
    step = pl.program_id(0)

    @pl.when(step == 0)
    def _():
        gram_ref[...] = gram

    @pl.when(step > 0)
    def _():
        gram_ref[...] += gram

    @pl.when(step == pl.num_programs(0) - 1)
    def _():
        bit = me_x & 1
        for j in range(nx // 2):
            mine = pl.multiple_of((2 * j + bit) * x_local, x_local)
            other = pl.multiple_of((2 * j + 1 - bit) * x_local, x_local)
            keep_ref[j] = gram_ref[pl.ds(mine, x_local), :]
            sent_ref[j] = gram_ref[pl.ds(other, x_local), :]


def gram_x_terms(sizes, where, flat, parts):
    nx = sizes[0]
    own, x_local, y_local = parts[0].shape
    width = nx * x_local
    batch = 4
    field = (batch, x_local, y_local)
    specs = [pl.BlockSpec(field, lambda i, s: (s[0] * own // batch + i, 0, 0))]
    specs += [pl.BlockSpec(field, lambda i, s: (i, 0, 0))] * (nx - 1)
    half = (nx // 2, x_local, width)
    flops = 2 * own * y_local * width * width * 3
    return pl.pallas_call(
        functools.partial(gram_x_kernel, sizes),
        grid_spec=pltpu.PrefetchScalarGridSpec(
            num_scalar_prefetch=1,
            grid=(own // batch,),
            in_specs=specs,
            out_specs=[whole_spec(half)] * 2,
            scratch_shapes=[pltpu.VMEM((width, batch * y_local), F32), pltpu.VMEM((width, width), F32)],
        ),
        out_shape=[jax.ShapeDtypeStruct(half, F32)] * 2,
        compiler_params=params(),
        cost_estimate=pl.CostEstimate(flops=flops, bytes_accessed=1 << 23, transcendentals=0),
    )(where, flat, *parts)


def unpack_kernel(ny, own, starts, s_ref, *refs):
    parts, out_ref = refs[:-1], refs[-1]
    b_block = out_ref.shape[2]
    for c, start in enumerate(starts):
        for k in range(ny):
            part = parts[c * ny + k]
            for j in range(part.shape[0]):
                base = (s_ref[1] ^ k) * own + start + 2 * j
                out_ref[base] = part[j, :, :b_block]
                out_ref[base + 1] = part[j, :, b_block:]


def unpack(sizes, where, parts, starts, rows):
    ny = sizes[1]
    _, a_block, lanes = parts[0].shape
    shape = (rows, a_block, lanes // 2)
    return pl.pallas_call(
        functools.partial(unpack_kernel, ny, rows // ny, starts),
        grid_spec=pltpu.PrefetchScalarGridSpec(
            num_scalar_prefetch=1,
            grid=(1,),
            in_specs=[whole_spec(p.shape) for p in parts],
            out_specs=whole_spec(shape),
        ),
        out_shape=jax.ShapeDtypeStruct(shape, F32),
        compiler_params=params(),
        cost_estimate=pl.CostEstimate(flops=1000, bytes_accessed=3 << 20, transcendentals=0),
    )(where, *parts)


def local_step(slab, factor_x, factor_y):
    z_cells, s_local, x_local, y_local = slab.shape
    sizes = nx, ny, ns = tuple(lax.axis_size(a) for a in ("gx", "gy", "sa"))
    me_x, me_y, me_s = (lax.axis_index(a) for a in ("gx", "gy", "sa"))
    where = jnp.stack([me_x, me_y, me_s]).astype(jnp.int32)
    rank = factor_x.shape[1]
    a_block, b_block = rank // nx, rank // ny
    rows = z_cells * s_local
    flat = slab.reshape((rows, x_local, y_local))
    own_y, own_x = rows // ny, rows // nx
    counts = chunk_sizes(own_y)
    starts = [sum(counts[:c]) for c in range(len(counts))]
    x_total, y_total, s_total = x_local * nx, y_local * ny, s_local * ns

    keys = [[(1, k, own_y, starts[c], counts[c]) for k in range(ny)] for c in range(len(counts))]
    x_keys = [(0, k, own_x, 0, own_x) for k in range(1, nx)]
    groups = [keys[0][1:], x_keys, [keys[0][0]] + sum(keys[1:], [])]
    pieces = {}
    for group in groups:
        pieces.update(zip(group, cut(where, flat, group)))
    along_y = []
    for c in range(len(counts)):
        here = [pieces[keys[c][0]]]
        here += [swap(pieces[keys[c][k]], "gy", k) for k in range(1, ny)]
        along_y.append(here)
    along_x = [swap(pieces[x_keys[k - 1]], "gx", k) for k in range(1, nx)]
    mine = pick(factor_y.reshape((nx, y_local // nx, rank)), me_x, 0)
    crossed = jnp.stack([swap(mine, "gy", k) for k in range(1, ny)])
    fy_parts = [crossed] + [swap(crossed, "gx", o) for o in range(1, nx)]
    fy = gather_fy(sizes, where, factor_y, fy_parts)
    fxt = factor_x.T

    gram = None
    core_parts = []
    for c in range(len(counts)):
        last = c == len(counts) - 1
        out = chunk_terms(sizes, where, along_y[c], fy, fxt, gram, last)
        keep, sent, gram = out[0], out[1], out[2:]
        if last:
            gkeep, gsent = gram
            ggot = swap(gsent, "gx", 1)
        else:
            gram = gram[0]
        bit = 1
        while bit < nx:
            got = swap(sent, "gx", bit)
            if 2 * bit < nx:
                sent = keep[1::2] + got[1::2]
                keep, got = keep[0::2], got[0::2]
            keep = keep + got
            bit *= 2
        keep = keep[0]
        z_parts = [pick(keep, me_y ^ k, 0) for k in range(ny)]
        core_parts += [swap(z_parts[k], "gy", k) if k else z_parts[0] for k in range(ny)]
    core = unpack(sizes, where, core_parts, starts, rows)
    core = core.reshape((z_cells, s_local, a_block, b_block))

    keep, sent = gram_x_terms(sizes, where, flat, along_x)
    got = swap(sent, "gx", 1)
    bit = 2
    while bit < nx:
        keep = keep.reshape((-1, 2, x_local, x_total))
        got = got.reshape((-1, 2, x_local, x_total))
        mybit = (me_x // bit) & 1
        sent = pick(keep, 1 - mybit, 1) + pick(got, 1 - mybit, 1)
        keep = pick(keep, mybit, 1) + pick(got, mybit, 1)
        got = swap(sent, "gx", bit)
        bit *= 2
    total = (keep[0] + got[0]).reshape((ny, ns, -1, x_total))
    keep = pick(total, me_s, 1)
    for k in range(1, ns):
        keep = keep + swap(pick(total, me_s ^ k, 1), "sa", k)
    gram_x = pick(keep, me_y, 0)
    for k in range(1, ny):
        gram_x = gram_x + swap(pick(keep, me_y ^ k, 0), "gy", k)
    gram_x = gram_x / (y_total * z_cells * s_total)

    keep, got = gkeep, ggot
    bit = 2
    while bit < nx:
        shape = (ny, 2, keep.shape[1] // 2, y_total)
        keep, got = keep.reshape(shape), got.reshape(shape)
        mybit = (me_x // bit) & 1
        sent = pick(keep, 1 - mybit, 1) + pick(got, 1 - mybit, 1)
        keep = pick(keep, mybit, 1) + pick(got, mybit, 1)
        got = swap(sent, "gx", bit)
        bit *= 2
    total = keep + got
    row = pick(total, me_y, 0)
    for k in range(1, ny):
        row = row + swap(pick(total, me_y ^ k, 0), "gy", k)
    summed = row
    for k in range(1, ns):
        summed = summed + swap(row, "sa", k)
    parts = [summed] + [swap(summed, "gx", o) for o in range(1, nx)]
    gram_y = place_rows(where, parts, x_total * z_cells * s_total)
    return (gram_x, gram_y, core)


def solution(mesh):
    in_specs = (P(None, "sa", "gx", "gy"), P("gx", None), P("gy", None))
    out_specs = (P(("gx", "gy", "sa"), None), P("gy", None), P(None, "sa", "gx", "gy"))
    return jax.shard_map(
        local_step, mesh=mesh, in_specs=in_specs, out_specs=out_specs, check_vma=False
    )
```

```python
import functools
import math

import jax
import jax.numpy as jnp
from jax import lax
from jax.experimental import pallas as pl
from jax.experimental.pallas import tpu as pltpu
from jax.sharding import PartitionSpec as P


F32 = jnp.float32
BF16 = jnp.bfloat16
ROWS = (((0,), (0,)), ((), ()))
LANES = (((1,), (1,)), ((), ()))
PLAIN = (((1,), (0,)), ((), ()))


def swap(value, axis, offset):
    size = lax.axis_size(axis)
    return lax.ppermute(value, axis, [(i, i ^ offset) for i in range(size)])


def early_shift(size):
    return size // 2


def pick(value, index, axis):
    return lax.dynamic_index_in_dim(value, index, axis, keepdims=False)


def split(value):
    high = value.astype(BF16)
    return high, (value - high.astype(F32)).astype(BF16)


def dot3(left, right, dims):
    (lc,), (rc,) = dims[0]
    lhs = jnp.concatenate([left[0], left[0], left[1]], axis=lc)
    rhs = jnp.concatenate([right[0], right[1], right[0]], axis=rc)
    return lax.dot_general(lhs, rhs, dims, preferred_element_type=F32)


def params():
    return pltpu.CompilerParams(vmem_limit_bytes=24 << 20)


def piece_sizes(own):
    sizes = (own // 4,) * 4
    assert all(n > 0 and n % 2 == 0 for n in sizes)
    return sizes, ((0, 1), (2,), (3,))


def whole_spec(shape):
    return pl.BlockSpec(shape, lambda i, s: (0,) * len(shape))


def cut_kernel(s_ref, *refs):
    half = len(refs) // 2
    for source, target in zip(refs[:half], refs[half:]):
        target[...] = source[...]


def cut(where, flat, pieces):
    unit = math.gcd(4, *[n for _, _, *counts in pieces for n in counts])
    block = (unit,) + flat.shape[1:]
    steps = max(size for *_, size in pieces) // unit
    in_specs, out_specs, out_shape = [], [], []
    for axis, k, own, start, size in pieces:

        def source(i, s, axis=axis, k=k, own=own, start=start, size=size):
            first = ((s[axis] ^ k) * own + start) // unit
            return (first + jnp.minimum(i, size // unit - 1), 0, 0)

        def target(i, s, size=size):
            return (jnp.minimum(i, size // unit - 1), 0, 0)

        in_specs.append(pl.BlockSpec(block, source))
        out_specs.append(pl.BlockSpec(block, target))
        out_shape.append(jax.ShapeDtypeStruct((size,) + flat.shape[1:], F32))
    return pl.pallas_call(
        cut_kernel,
        grid_spec=pltpu.PrefetchScalarGridSpec(
            num_scalar_prefetch=1, grid=(steps,), in_specs=in_specs, out_specs=out_specs
        ),
        out_shape=out_shape,
        cost_estimate=pl.CostEstimate(flops=1000, bytes_accessed=1 << 22, transcendentals=0),
    )(where, *[flat] * len(pieces))


def reverse_bits(value, count):
    bits = count.bit_length() - 1
    return sum(((value >> i) & 1) << (bits - 1 - i) for i in range(bits))


def rows_kernel(terms, s_ref, *refs):
    parts, out_ref = refs[:-1], refs[-1]
    size = parts[0].shape[0]
    for o, part in enumerate(parts):
        place = reverse_bits(s_ref[0] ^ o, len(parts))
        out_ref[pl.ds(pl.multiple_of(place * size, size), size), :] = part[...] / terms


def place_rows(where, parts, terms):
    size, width = parts[0].shape
    shape = (len(parts) * size, width)
    return pl.pallas_call(
        functools.partial(rows_kernel, terms),
        grid_spec=pltpu.PrefetchScalarGridSpec(
            num_scalar_prefetch=1,
            grid=(1,),
            in_specs=[whole_spec((size, width))] * len(parts),
            out_specs=whole_spec(shape),
        ),
        out_shape=jax.ShapeDtypeStruct(shape, F32),
        compiler_params=params(),
        cost_estimate=pl.CostEstimate(flops=1000, bytes_accessed=1 << 19, transcendentals=0),
    )(where, *parts)


def fy_kernel(ny, nx, s_ref, own_ref, *refs):
    pieces, (high_ref, low_ref, scratch) = refs[:nx], refs[nx:]
    depth = own_ref.shape[0]
    small = depth // nx
    scratch[pl.ds(pl.multiple_of(s_ref[1] * depth, depth), depth), :] = own_ref[...]
    for o in range(nx):
        for k in range(1, ny):
            start = (s_ref[1] ^ k) * depth + (s_ref[0] ^ o) * small
            scratch[pl.ds(pl.multiple_of(start, small), small), :] = pieces[o][k - 1]
    high_ref[...], low_ref[...] = split(scratch[...])


def gather_fy(sizes, where, factor_y, pieces):
    nx, ny = sizes[:2]
    depth, rank = factor_y.shape
    shape = (ny * depth, rank)
    return pl.pallas_call(
        functools.partial(fy_kernel, ny, nx),
        grid_spec=pltpu.PrefetchScalarGridSpec(
            num_scalar_prefetch=1,
            grid=(1,),
            in_specs=[whole_spec(factor_y.shape)] + [whole_spec(p.shape) for p in pieces],
            out_specs=[whole_spec(shape)] * 2,
            scratch_shapes=[pltpu.VMEM(shape, F32)],
        ),
        out_shape=[jax.ShapeDtypeStruct(shape, BF16)] * 2,
        compiler_params=params(),
        cost_estimate=pl.CostEstimate(flops=1000, bytes_accessed=1 << 20, transcendentals=0),
    )(where, factor_y, *pieces)


def chunk_kernel(sizes, count, first, last, s_ref, *refs):
    nx, ny, _ = sizes
    fields, refs = refs[: count * ny], refs[count * ny :]
    (fyh_ref, fyl_ref, fxt_ref), refs = refs[:3], refs[3:]
    if not first:
        gin_ref, refs = refs[0], refs[1:]
    keep_ref, sent_ref, refs = refs[0], refs[1], refs[2:]
    if last:
        gkeep_ref, gsent_ref, wide_ref, gram_ref = refs
    else:
        gram_ref, wide_ref = refs
    _, x_local, y_local = fields[0].shape
    me_x, me_y = s_ref[0], s_ref[1]
    n = wide_ref.shape[0] // x_local
    for k in range(ny):
        start = pl.multiple_of((me_y ^ k) * y_local, y_local)
        row = 0
        for p in range(count):
            part = fields[p * ny + k]
            rows = part.shape[0] * x_local
            wide_ref[row : row + rows, pl.ds(start, y_local)] = part[...].reshape(rows, y_local)
            row += rows
    wide = split(wide_ref[...])
    gram = dot3(wide, wide, ROWS)
    gram_ref[...] = gram if first else gin_ref[...] + gram

    half = dot3(wide, (fyh_ref[...], fyl_ref[...]), PLAIN)
    b_block = half.shape[1] // ny
    paired = jnp.concatenate(
        [
            half[p * x_local : (p + 1) * x_local, q * b_block : (q + 1) * b_block]
            for j in range(n // 2)
            for q in range(ny)
            for p in (2 * j, 2 * j + 1)
        ],
        axis=1,
    )
    a_block = fxt_ref.shape[0] // nx
    fx = jnp.concatenate(
        [
            fxt_ref[pl.ds(pl.multiple_of((me_x ^ o) * a_block, a_block), a_block), :]
            for o in range(nx)
        ],
        axis=0,
    )
    full = dot3(split(fx), split(paired), PLAIN)
    lanes = 2 * b_block
    for o in range(nx):
        target = sent_ref if o % 2 else keep_ref
        for j in range(n // 2):
            for q in range(ny):
                at = (j * ny + q) * lanes
                target[o // 2, q, j] = full[o * a_block : (o + 1) * a_block, at : at + lanes]
    if last:
        part = y_local // 2
        bit = me_x & 1
        for k in range(ny):
            mine = pl.multiple_of(k * y_local + bit * part, part)
            other = pl.multiple_of(k * y_local + (1 - bit) * part, part)
            gkeep_ref[k] = gram_ref[pl.ds(mine, part), :]
            gsent_ref[k] = gram_ref[pl.ds(other, part), :]


def chunk_terms(sizes, where, parts, fy, fxt, gram, last):
    nx, ny, _ = sizes
    _, x_local, y_local = parts[0].shape
    count = len(parts) // ny
    n = sum(part.shape[0] for part in parts[::ny])
    rank = fxt.shape[0]
    pairs = n // 2
    width = ny * y_local
    a_block, b_block = rank // nx, rank // ny
    half = (nx // 2, ny, pairs, a_block, 2 * b_block)
    specs = [whole_spec(part.shape) for part in parts]
    specs += [whole_spec(fy[0].shape)] * 2 + [whole_spec(fxt.shape)]
    args = [*parts, *fy, fxt]
    first = gram is None
    if not first:
        specs.append(whole_spec((width, width)))
        args.append(gram)
    out_specs = [whole_spec(half)] * 2
    out_shape = [jax.ShapeDtypeStruct(half, F32)] * 2
    scratch = [pltpu.VMEM((n * x_local, width), F32)]
    if last:
        gshape = (ny, y_local // 2, width)
        out_specs += [whole_spec(gshape)] * 2
        out_shape += [jax.ShapeDtypeStruct(gshape, F32)] * 2
        scratch.append(pltpu.VMEM((width, width), F32))
    else:
        out_specs.append(whole_spec((width, width)))
        out_shape.append(jax.ShapeDtypeStruct((width, width), F32))
    flops = 2 * n * x_local * (width * width + width * rank + rank * rank) * 3
    return pl.pallas_call(
        functools.partial(chunk_kernel, sizes, count, first, last),
        grid_spec=pltpu.PrefetchScalarGridSpec(
            num_scalar_prefetch=1,
            grid=(1,),
            in_specs=specs,
            out_specs=out_specs,
            scratch_shapes=scratch,
        ),
        out_shape=out_shape,
        compiler_params=params(),
        cost_estimate=pl.CostEstimate(flops=flops, bytes_accessed=1 << 22, transcendentals=0),
    )(where, *args)


def gram_x_kernel(sizes, s_ref, *refs):
    nx = sizes[0]
    fields, (keep_ref, sent_ref, tall_ref, gram_ref) = refs[:nx], refs[nx:]
    pair, x_local, y_local = fields[0].shape
    me_x = s_ref[0]
    for o in range(nx):
        start = pl.multiple_of((me_x ^ o) * x_local, x_local)
        for p in range(pair):
            tall_ref[pl.ds(start, x_local), p * y_local : (p + 1) * y_local] = fields[o][p]
    tall = split(tall_ref[...])
    gram = dot3(tall, tall, LANES)
    step = pl.program_id(0)

    @pl.when(step == 0)
    def _():
        gram_ref[...] = gram

    @pl.when(step > 0)
    def _():
        gram_ref[...] += gram

    @pl.when(step == pl.num_programs(0) - 1)
    def _():
        bit = me_x & 1
        for j in range(nx // 2):
            mine = pl.multiple_of((2 * j + bit) * x_local, x_local)
            other = pl.multiple_of((2 * j + 1 - bit) * x_local, x_local)
            keep_ref[j] = gram_ref[pl.ds(mine, x_local), :]
            sent_ref[j] = gram_ref[pl.ds(other, x_local), :]


def gram_x_terms(sizes, where, flat, parts):
    nx = sizes[0]
    own, x_local, y_local = parts[0].shape
    width = nx * x_local
    batch = 4
    field = (batch, x_local, y_local)
    specs = [pl.BlockSpec(field, lambda i, s: (s[0] * own // batch + i, 0, 0))]
    specs += [pl.BlockSpec(field, lambda i, s: (i, 0, 0))] * (nx - 1)
    half = (nx // 2, x_local, width)
    flops = 2 * own * y_local * width * width * 3
    return pl.pallas_call(
        functools.partial(gram_x_kernel, sizes),
        grid_spec=pltpu.PrefetchScalarGridSpec(
            num_scalar_prefetch=1,
            grid=(own // batch,),
            in_specs=specs,
            out_specs=[whole_spec(half)] * 2,
            scratch_shapes=[pltpu.VMEM((width, batch * y_local), F32), pltpu.VMEM((width, width), F32)],
        ),
        out_shape=[jax.ShapeDtypeStruct(half, F32)] * 2,
        compiler_params=params(),
        cost_estimate=pl.CostEstimate(flops=flops, bytes_accessed=1 << 23, transcendentals=0),
    )(where, flat, *parts)


def unpack_kernel(ny, own, starts, s_ref, *refs):
    parts, out_ref = refs[:-1], refs[-1]
    b_block = out_ref.shape[2]
    for c, start in enumerate(starts):
        for k in range(ny):
            part = parts[c * ny + k]
            for j in range(part.shape[0]):
                base = (s_ref[1] ^ k) * own + start + 2 * j
                out_ref[base] = part[j, :, :b_block]
                out_ref[base + 1] = part[j, :, b_block:]


def unpack(sizes, where, parts, starts, rows):
    ny = sizes[1]
    _, a_block, lanes = parts[0].shape
    shape = (rows, a_block, lanes // 2)
    return pl.pallas_call(
        functools.partial(unpack_kernel, ny, rows // ny, starts),
        grid_spec=pltpu.PrefetchScalarGridSpec(
            num_scalar_prefetch=1,
            grid=(1,),
            in_specs=[whole_spec(p.shape) for p in parts],
            out_specs=whole_spec(shape),
        ),
        out_shape=jax.ShapeDtypeStruct(shape, F32),
        compiler_params=params(),
        cost_estimate=pl.CostEstimate(flops=1000, bytes_accessed=3 << 20, transcendentals=0),
    )(where, *parts)


def local_step(slab, factor_x, factor_y):
    z_cells, s_local, x_local, y_local = slab.shape
    sizes = nx, ny, ns = tuple(lax.axis_size(a) for a in ("gx", "gy", "sa"))
    me_x, me_y, me_s = (lax.axis_index(a) for a in ("gx", "gy", "sa"))
    where = jnp.stack([me_x, me_y, me_s]).astype(jnp.int32)
    rank = factor_x.shape[1]
    a_block, b_block = rank // nx, rank // ny
    rows = z_cells * s_local
    flat = slab.reshape((rows, x_local, y_local))
    own_y, own_x = rows // ny, rows // nx
    counts, chunks = piece_sizes(own_y)
    starts = [sum(counts[:c]) for c in range(len(counts))]
    x_total, y_total, s_total = x_local * nx, y_local * ny, s_local * ns

    keys = [[(1, k, own_y, starts[c], counts[c]) for k in range(ny)] for c in range(len(counts))]
    x_keys = [(0, k, own_x, 0, own_x) for k in range(1, nx)]
    own_keys = [key[0] for key in keys]
    early = early_shift(nx)
    groups = [keys[0][1:], [x_keys[early - 1]], keys[1][1:] + own_keys[:2]]
    groups += [keys[2] + keys[3], [key for key in x_keys if key[1] != early]]
    pieces = {}
    for group in groups:
        pieces.update(zip(group, cut(where, flat, group)))
    along_y = []
    for c in range(len(counts)):
        here = [pieces[keys[c][0]]]
        here += [swap(pieces[keys[c][k]], "gy", k) for k in range(1, ny)]
        along_y.append(here)
    along_x = [swap(pieces[x_keys[k - 1]], "gx", k) for k in range(1, nx)]
    mine = pick(factor_y.reshape((nx, y_local // nx, rank)), me_x, 0)
    crossed = jnp.stack([swap(mine, "gy", k) for k in range(1, ny)])
    fy_parts = [crossed] + [swap(crossed, "gx", o) for o in range(1, nx)]
    fy = gather_fy(sizes, where, factor_y, fy_parts)
    fxt = factor_x.T

    gram = None
    core_parts = []
    for c, members in enumerate(chunks):
        last = c == len(chunks) - 1
        parts = sum((along_y[p] for p in members), [])
        out = chunk_terms(sizes, where, parts, fy, fxt, gram, last)
        keep, sent, gram = out[0], out[1], out[2:]
        if last:
            gkeep, gsent = gram
            ggot = swap(gsent, "gx", 1)
        else:
            gram = gram[0]
        bit = 1
        while bit < nx:
            got = swap(sent, "gx", bit)
            if 2 * bit < nx:
                sent = keep[1::2] + got[1::2]
                keep, got = keep[0::2], got[0::2]
            keep = keep + got
            bit *= 2
        keep = keep[0]
        z_parts = [pick(keep, me_y ^ k, 0) for k in range(ny)]
        core_parts += [swap(z_parts[k], "gy", k) if k else z_parts[0] for k in range(ny)]
    core = unpack(sizes, where, core_parts, [starts[m[0]] for m in chunks], rows)
    core = core.reshape((z_cells, s_local, a_block, b_block))

    keep, sent = gram_x_terms(sizes, where, flat, along_x)
    got = swap(sent, "gx", 1)
    bit = 2
    while bit < nx:
        keep = keep.reshape((-1, 2, x_local, x_total))
        got = got.reshape((-1, 2, x_local, x_total))
        mybit = (me_x // bit) & 1
        sent = pick(keep, 1 - mybit, 1) + pick(got, 1 - mybit, 1)
        keep = pick(keep, mybit, 1) + pick(got, mybit, 1)
        got = swap(sent, "gx", bit)
        bit *= 2
    total = (keep[0] + got[0]).reshape((ny, ns, -1, x_total))
    keep = pick(total, me_s, 1)
    for k in range(1, ns):
        keep = keep + swap(pick(total, me_s ^ k, 1), "sa", k)
    gram_x = pick(keep, me_y, 0)
    for k in range(1, ny):
        gram_x = gram_x + swap(pick(keep, me_y ^ k, 0), "gy", k)
    gram_x = gram_x / (y_total * z_cells * s_total)

    keep, got = gkeep, ggot
    bit = 2
    while bit < nx:
        shape = (ny, 2, keep.shape[1] // 2, y_total)
        keep, got = keep.reshape(shape), got.reshape(shape)
        mybit = (me_x // bit) & 1
        sent = pick(keep, 1 - mybit, 1) + pick(got, 1 - mybit, 1)
        keep = pick(keep, mybit, 1) + pick(got, mybit, 1)
        got = swap(sent, "gx", bit)
        bit *= 2
    total = keep + got
    row = pick(total, me_y, 0)
    for k in range(1, ny):
        row = row + swap(pick(total, me_y ^ k, 0), "gy", k)
    summed = row
    for k in range(1, ns):
        summed = summed + swap(row, "sa", k)
    parts = [summed] + [swap(summed, "gx", o) for o in range(1, nx)]
    gram_y = place_rows(where, parts, x_total * z_cells * s_total)
    return (gram_x, gram_y, core)


def solution(mesh):
    in_specs = (P(None, "sa", "gx", "gy"), P("gx", None), P("gy", None))
    out_specs = (P(("gx", "gy", "sa"), None), P("gy", None), P(None, "sa", "gx", "gy"))
    return jax.shard_map(
        local_step, mesh=mesh, in_specs=in_specs, out_specs=out_specs, check_vma=False
    )
```

```python
import functools
import math

import jax
import jax.numpy as jnp
from jax import lax
from jax.experimental import pallas as pl
from jax.experimental.pallas import tpu as pltpu
from jax.sharding import PartitionSpec as P


F32 = jnp.float32
BF16 = jnp.bfloat16
ROWS = (((0,), (0,)), ((), ()))
LANES = (((1,), (1,)), ((), ()))
PLAIN = (((1,), (0,)), ((), ()))


def swap(value, axis, offset):
    size = lax.axis_size(axis)
    return lax.ppermute(value, axis, [(i, i ^ offset) for i in range(size)])


def early_shift(size):
    return size // 2


def pick(value, index, axis):
    return lax.dynamic_index_in_dim(value, index, axis, keepdims=False)


def split(value):
    high = value.astype(BF16)
    return high, (value - high.astype(F32)).astype(BF16)


def dot3(left, right, dims):
    (lc,), (rc,) = dims[0]
    lhs = jnp.concatenate([left[0], left[0], left[1]], axis=lc)
    rhs = jnp.concatenate([right[0], right[1], right[0]], axis=rc)
    return lax.dot_general(lhs, rhs, dims, preferred_element_type=F32)


def params():
    return pltpu.CompilerParams(vmem_limit_bytes=48 << 20)


def piece_sizes(own):
    sizes = (own // 4,) * 4
    assert all(n > 0 and n % 2 == 0 for n in sizes)
    return sizes, ((0,), (1,), (2,), (3,)), ((0, 1), (2,), (3,))


def in_hbm(arrays):
    return [pltpu.with_memory_space_constraint(a, pltpu.HBM) for a in arrays]


def whole_spec(shape):
    return pl.BlockSpec(shape, lambda i, s: (0,) * len(shape))


def cut_kernel(s_ref, *refs):
    half = len(refs) // 2
    for source, target in zip(refs[:half], refs[half:]):
        target[...] = source[...]


def cut(where, flat, pieces):
    unit = math.gcd(*[n for _, _, *counts in pieces for n in counts if n])
    block = (unit,) + flat.shape[1:]
    steps = max(size for *_, size in pieces) // unit
    in_specs, out_specs, out_shape = [], [], []
    for axis, k, own, start, size in pieces:

        def source(i, s, axis=axis, k=k, own=own, start=start, size=size):
            first = ((s[axis] ^ k) * own + start) // unit
            return (first + jnp.minimum(i, size // unit - 1), 0, 0)

        def target(i, s, size=size):
            return (jnp.minimum(i, size // unit - 1), 0, 0)

        in_specs.append(pl.BlockSpec(block, source))
        out_specs.append(pl.BlockSpec(block, target))
        out_shape.append(jax.ShapeDtypeStruct((size,) + flat.shape[1:], F32))
    return pl.pallas_call(
        cut_kernel,
        grid_spec=pltpu.PrefetchScalarGridSpec(
            num_scalar_prefetch=1, grid=(steps,), in_specs=in_specs, out_specs=out_specs
        ),
        out_shape=out_shape,
        cost_estimate=pl.CostEstimate(flops=1000, bytes_accessed=1 << 22, transcendentals=0),
    )(where, *[flat] * len(pieces))


def reverse_bits(value, count):
    bits = count.bit_length() - 1
    return sum(((value >> i) & 1) << (bits - 1 - i) for i in range(bits))


def rows_kernel(terms, s_ref, *refs):
    parts, out_ref = refs[:-1], refs[-1]
    size = parts[0].shape[0]
    for o, part in enumerate(parts):
        place = reverse_bits(s_ref[0] ^ o, len(parts))
        out_ref[pl.ds(pl.multiple_of(place * size, size), size), :] = part[...] / terms


def place_rows(where, parts, terms):
    size, width = parts[0].shape
    shape = (len(parts) * size, width)
    return pl.pallas_call(
        functools.partial(rows_kernel, terms),
        grid_spec=pltpu.PrefetchScalarGridSpec(
            num_scalar_prefetch=1,
            grid=(1,),
            in_specs=[whole_spec((size, width))] * len(parts),
            out_specs=whole_spec(shape),
        ),
        out_shape=jax.ShapeDtypeStruct(shape, F32),
        compiler_params=params(),
        cost_estimate=pl.CostEstimate(flops=1000, bytes_accessed=1 << 19, transcendentals=0),
    )(where, *parts)


def fy_kernel(ny, nx, s_ref, own_ref, *refs):
    pieces, (high_ref, low_ref, scratch) = refs[:nx], refs[nx:]
    depth = own_ref.shape[0]
    small = depth // nx
    scratch[pl.ds(pl.multiple_of(s_ref[1] * depth, depth), depth), :] = own_ref[...]
    for o in range(nx):
        for k in range(1, ny):
            start = (s_ref[1] ^ k) * depth + (s_ref[0] ^ o) * small
            scratch[pl.ds(pl.multiple_of(start, small), small), :] = pieces[o][k - 1]
    high_ref[...], low_ref[...] = split(scratch[...])


def gather_fy(sizes, where, factor_y, pieces):
    nx, ny = sizes[:2]
    depth, rank = factor_y.shape
    shape = (ny * depth, rank)
    return pl.pallas_call(
        functools.partial(fy_kernel, ny, nx),
        grid_spec=pltpu.PrefetchScalarGridSpec(
            num_scalar_prefetch=1,
            grid=(1,),
            in_specs=[whole_spec(factor_y.shape)] + [whole_spec(p.shape) for p in pieces],
            out_specs=[whole_spec(shape)] * 2,
            scratch_shapes=[pltpu.VMEM(shape, F32)],
        ),
        out_shape=[jax.ShapeDtypeStruct(shape, BF16)] * 2,
        compiler_params=params(),
        cost_estimate=pl.CostEstimate(flops=1000, bytes_accessed=1 << 20, transcendentals=0),
    )(where, factor_y, *pieces)


def chunk_kernel(sizes, count, first, last, s_ref, *refs):
    nx, ny, _ = sizes
    fields, refs = refs[: count * ny], refs[count * ny :]
    (fyh_ref, fyl_ref, fxt_ref), refs = refs[:3], refs[3:]
    if not first:
        gin_ref, refs = refs[0], refs[1:]
    keep_ref, sent_ref, refs = refs[0], refs[1], refs[2:]
    if last:
        gkeep_ref, gsent_ref, wide_ref, gram_ref = refs
    else:
        gram_ref, wide_ref = refs
    _, x_local, y_local = fields[0].shape
    me_x, me_y = s_ref[0], s_ref[1]
    n = wide_ref.shape[0] // x_local
    for k in range(ny):
        start = pl.multiple_of((me_y ^ k) * y_local, y_local)
        row = 0
        for p in range(count):
            part = fields[p * ny + k]
            rows = part.shape[0] * x_local
            wide_ref[row : row + rows, pl.ds(start, y_local)] = part[...].reshape(rows, y_local)
            row += rows
    wide = split(wide_ref[...])
    gram = dot3(wide, wide, ROWS)
    gram_ref[...] = gram if first else gin_ref[...] + gram

    half = dot3(wide, (fyh_ref[...], fyl_ref[...]), PLAIN)
    b_block = half.shape[1] // ny
    paired = jnp.concatenate(
        [
            half[p * x_local : (p + 1) * x_local, q * b_block : (q + 1) * b_block]
            for j in range(n // 2)
            for q in range(ny)
            for p in (2 * j, 2 * j + 1)
        ],
        axis=1,
    )
    a_block = fxt_ref.shape[0] // nx
    fx = jnp.concatenate(
        [
            fxt_ref[pl.ds(pl.multiple_of((me_x ^ o) * a_block, a_block), a_block), :]
            for o in range(nx)
        ],
        axis=0,
    )
    full = dot3(split(fx), split(paired), PLAIN)
    lanes = 2 * b_block
    for o in range(nx):
        target = sent_ref if o % 2 else keep_ref
        for j in range(n // 2):
            for q in range(ny):
                at = (j * ny + q) * lanes
                target[o // 2, q, j] = full[o * a_block : (o + 1) * a_block, at : at + lanes]
    if last:
        part = y_local // 2
        bit = me_x & 1
        for k in range(ny):
            mine = pl.multiple_of(k * y_local + bit * part, part)
            other = pl.multiple_of(k * y_local + (1 - bit) * part, part)
            gkeep_ref[k] = gram_ref[pl.ds(mine, part), :]
            gsent_ref[k] = gram_ref[pl.ds(other, part), :]


def chunk_terms(sizes, where, parts, fy, fxt, gram, last):
    nx, ny, _ = sizes
    _, x_local, y_local = parts[0].shape
    count = len(parts) // ny
    n = sum(part.shape[0] for part in parts[::ny])
    rank = fxt.shape[0]
    pairs = n // 2
    width = ny * y_local
    a_block, b_block = rank // nx, rank // ny
    half = (nx // 2, ny, pairs, a_block, 2 * b_block)
    specs = [whole_spec(part.shape) for part in parts]
    specs += [whole_spec(fy[0].shape)] * 2 + [whole_spec(fxt.shape)]
    args = [*in_hbm(parts), *fy, fxt]
    first = gram is None
    if not first:
        specs.append(whole_spec((width, width)))
        args += in_hbm([gram])
    out_specs = [whole_spec(half)] * 2
    out_shape = [jax.ShapeDtypeStruct(half, F32)] * 2
    scratch = [pltpu.VMEM((n * x_local, width), F32)]
    if last:
        gshape = (ny, y_local // 2, width)
        out_specs += [whole_spec(gshape)] * 2
        out_shape += [jax.ShapeDtypeStruct(gshape, F32)] * 2
        scratch.append(pltpu.VMEM((width, width), F32))
    else:
        out_specs.append(whole_spec((width, width)))
        out_shape.append(pltpu.HBM((width, width), F32))
    flops = 2 * n * x_local * (width * width + width * rank + rank * rank) * 3
    return pl.pallas_call(
        functools.partial(chunk_kernel, sizes, count, first, last),
        grid_spec=pltpu.PrefetchScalarGridSpec(
            num_scalar_prefetch=1,
            grid=(1,),
            in_specs=specs,
            out_specs=out_specs,
            scratch_shapes=scratch,
        ),
        out_shape=out_shape,
        compiler_params=params(),
        cost_estimate=pl.CostEstimate(flops=flops, bytes_accessed=1 << 22, transcendentals=0),
    )(where, *args)


def gram_x_kernel(sizes, s_ref, *refs):
    nx = sizes[0]
    fields, (keep_ref, sent_ref, tall_ref, gram_ref) = refs[:nx], refs[nx:]
    pair, x_local, y_local = fields[0].shape
    me_x = s_ref[0]
    for o in range(nx):
        start = pl.multiple_of((me_x ^ o) * x_local, x_local)
        for p in range(pair):
            tall_ref[pl.ds(start, x_local), p * y_local : (p + 1) * y_local] = fields[o][p]
    tall = split(tall_ref[...])
    gram = dot3(tall, tall, LANES)
    step = pl.program_id(0)

    @pl.when(step == 0)
    def _():
        gram_ref[...] = gram

    @pl.when(step > 0)
    def _():
        gram_ref[...] += gram

    @pl.when(step == pl.num_programs(0) - 1)
    def _():
        bit = me_x & 1
        for j in range(nx // 2):
            mine = pl.multiple_of((2 * j + bit) * x_local, x_local)
            other = pl.multiple_of((2 * j + 1 - bit) * x_local, x_local)
            keep_ref[j] = gram_ref[pl.ds(mine, x_local), :]
            sent_ref[j] = gram_ref[pl.ds(other, x_local), :]


def gram_x_terms(sizes, where, flat, parts):
    nx = sizes[0]
    own, x_local, y_local = parts[0].shape
    width = nx * x_local
    batch = 4
    field = (batch, x_local, y_local)
    specs = [pl.BlockSpec(field, lambda i, s: (s[0] * own // batch + i, 0, 0))]
    specs += [pl.BlockSpec(field, lambda i, s: (i, 0, 0))] * (nx - 1)
    half = (nx // 2, x_local, width)
    flops = 2 * own * y_local * width * width * 3
    return pl.pallas_call(
        functools.partial(gram_x_kernel, sizes),
        grid_spec=pltpu.PrefetchScalarGridSpec(
            num_scalar_prefetch=1,
            grid=(own // batch,),
            in_specs=specs,
            out_specs=[whole_spec(half)] * 2,
            scratch_shapes=[pltpu.VMEM((width, batch * y_local), F32), pltpu.VMEM((width, width), F32)],
        ),
        out_shape=[jax.ShapeDtypeStruct(half, F32)] * 2,
        compiler_params=params(),
        cost_estimate=pl.CostEstimate(flops=flops, bytes_accessed=1 << 23, transcendentals=0),
    )(where, *in_hbm([flat, *parts]))


def pack_kernel(ny, extra, s_ref, *refs):
    outs, refs = refs[-ny:], refs[:-ny]
    if extra:
        xrows, refs = refs[-1], refs[:-1]
    lanes = outs[0].shape[2]
    for k in range(ny):
        at = s_ref[1] ^ k
        row = 0
        for keep, got in zip(refs[::2], refs[1::2]):
            outs[k][row : row + keep.shape[1]] = keep[at] + got[at]
            row += keep.shape[1]
        if extra:
            size = xrows.shape[1]
            for j in range(xrows.shape[2] // lanes):
                block, start = divmod(j * size, outs[k].shape[1])
                outs[k][row + block, start : start + size] = xrows[
                    at, :, j * lanes : (j + 1) * lanes
                ]


def pack(sizes, where, halves, xrows=None):
    ny = sizes[1]
    args = [v for pair in halves for v in pair]
    _, _, a_block, lanes = args[0].shape
    count = sum(v.shape[1] for v in args[::2])
    if xrows is not None:
        args.append(xrows)
        count += xrows.shape[1] * xrows.shape[2] // (a_block * lanes)
    shape = (count, a_block, lanes)
    return pl.pallas_call(
        functools.partial(pack_kernel, ny, xrows is not None),
        grid_spec=pltpu.PrefetchScalarGridSpec(
            num_scalar_prefetch=1,
            grid=(1,),
            in_specs=[whole_spec(a.shape) for a in args],
            out_specs=[whole_spec(shape)] * ny,
        ),
        out_shape=[jax.ShapeDtypeStruct(shape, F32)] * ny,
        compiler_params=params(),
        cost_estimate=pl.CostEstimate(flops=1000, bytes_accessed=1 << 20, transcendentals=0),
    )(where, *args)


def unpack_kernel(ny, own, starts, counts, terms, s_ref, *refs):
    parts, (out_ref, gram_ref) = refs[:-2], refs[-2:]
    b_block = out_ref.shape[2]
    for c, start in enumerate(starts):
        for k in range(ny):
            part = parts[c * ny + k]
            for j in range(counts[c] // 2):
                base = (s_ref[1] ^ k) * own + start + 2 * j
                out_ref[base] = part[j, :, :b_block]
                out_ref[base + 1] = part[j, :, b_block:]
    size, lanes = gram_ref.shape[0], 2 * b_block
    for j in range(gram_ref.shape[1] // lanes):
        block, start = divmod(j * size, out_ref.shape[1])
        total = parts[0][counts[0] // 2 + block, start : start + size]
        for k in range(1, ny):
            total = total + parts[k][counts[0] // 2 + block, start : start + size]
        gram_ref[:, j * lanes : (j + 1) * lanes] = total / terms


def unpack(sizes, where, parts, starts, counts, rows, gram_shape, terms):
    ny = sizes[1]
    _, a_block, lanes = parts[0].shape
    shape = (rows, a_block, lanes // 2)
    return pl.pallas_call(
        functools.partial(unpack_kernel, ny, rows // ny, starts, counts, terms),
        grid_spec=pltpu.PrefetchScalarGridSpec(
            num_scalar_prefetch=1,
            grid=(1,),
            in_specs=[whole_spec(p.shape) for p in parts],
            out_specs=[whole_spec(shape), whole_spec(gram_shape)],
        ),
        out_shape=[jax.ShapeDtypeStruct(shape, F32), jax.ShapeDtypeStruct(gram_shape, F32)],
        compiler_params=params(),
        cost_estimate=pl.CostEstimate(flops=1000, bytes_accessed=3 << 20, transcendentals=0),
    )(where, *parts)


def local_step(slab, factor_x, factor_y):
    z_cells, s_local, x_local, y_local = slab.shape
    sizes = nx, ny, ns = tuple(lax.axis_size(a) for a in ("gx", "gy", "sa"))
    me_x, me_y, me_s = (lax.axis_index(a) for a in ("gx", "gy", "sa"))
    where = jnp.stack([me_x, me_y, me_s]).astype(jnp.int32)
    rank = factor_x.shape[1]
    a_block, b_block = rank // nx, rank // ny
    rows = z_cells * s_local
    flat = slab.reshape((rows, x_local, y_local))
    own_y, own_x = rows // ny, rows // nx
    counts, chunks, sends = piece_sizes(own_y)
    starts = [sum(counts[:c]) for c in range(len(counts))]
    x_total, y_total, s_total = x_local * nx, y_local * ny, s_local * ns

    keys = [[(1, k, own_y, starts[c], counts[c]) for k in range(ny)] for c in range(len(counts))]
    x_keys = [(0, k, own_x, 0, own_x) for k in range(1, nx)]
    own_keys = [key[0] for key in keys]
    early = early_shift(nx)
    groups = [keys[0][1:], [x_keys[early - 1]], keys[1][1:] + own_keys[:2]]
    groups += [keys[2] + keys[3], [key for key in x_keys if key[1] != early]]
    pieces = {}
    for group in groups:
        pieces.update(zip(group, cut(where, flat, group)))
    along_y = []
    for c in range(len(counts)):
        here = [pieces[keys[c][0]]]
        here += [swap(pieces[keys[c][k]], "gy", k) for k in range(1, ny)]
        along_y.append(here)
    along_x = [swap(pieces[x_keys[k - 1]], "gx", k) for k in range(1, nx)]
    mine = pick(factor_y.reshape((nx, y_local // nx, rank)), me_x, 0)
    crossed = jnp.stack([swap(mine, "gy", k) for k in range(1, ny)])
    fy_parts = [crossed] + [swap(crossed, "gx", o) for o in range(1, nx)]
    fy = gather_fy(sizes, where, factor_y, fy_parts)
    fxt = factor_x.T

    gram = None
    core_parts, reduced = [], []
    for c, members in enumerate(chunks):
        last = c == len(chunks) - 1
        parts = sum((along_y[p] for p in members), [])
        out = chunk_terms(sizes, where, parts, fy, fxt, gram, last)
        keep, sent, gram = out[0], out[1], out[2:]
        if last:
            gkeep, gsent = gram
            ggot = swap(gsent, "gx", 1)
        else:
            gram = gram[0]
        bit = 1
        while bit < nx:
            got = swap(sent, "gx", bit)
            if 2 * bit < nx:
                sent = keep[1::2] + got[1::2]
                keep, got = keep[0::2], got[0::2]
                keep = keep + got
            bit *= 2
        reduced.append((keep[0], got[0]))
    keep, sent = gram_x_terms(sizes, where, flat, along_x)
    got = swap(sent, "gx", 1)
    bit = 2
    while bit < nx:
        keep = keep.reshape((-1, 2, x_local, x_total))
        got = got.reshape((-1, 2, x_local, x_total))
        mybit = (me_x // bit) & 1
        sent = pick(keep, 1 - mybit, 1) + pick(got, 1 - mybit, 1)
        keep = pick(keep, mybit, 1) + pick(got, mybit, 1)
        got = swap(sent, "gx", bit)
        bit *= 2
    total = (keep[0] + got[0]).reshape((ny, ns, -1, x_total))
    x_rows = pick(total, me_s, 1)
    for k in range(1, ns):
        x_rows = x_rows + swap(pick(total, me_s ^ k, 1), "sa", k)

    for c, members in enumerate(sends):
        z_parts = pack(sizes, where, [reduced[m] for m in members], None if c else x_rows)
        core_parts += [swap(z_parts[k], "gy", k) if k else z_parts[0] for k in range(ny)]
    send_starts = [starts[chunks[m[0]][0]] for m in sends]
    send_counts = [sum(counts[p] for m in members for p in chunks[m]) for members in sends]
    gram_shape = x_rows.shape[1:]
    terms = y_total * z_cells * s_total
    core, gram_x = unpack(
        sizes, where, core_parts, send_starts, send_counts, rows, gram_shape, terms
    )
    core = core.reshape((z_cells, s_local, a_block, b_block))

    keep, got = gkeep, ggot
    bit = 2
    while bit < nx:
        shape = (ny, 2, keep.shape[1] // 2, y_total)
        keep, got = keep.reshape(shape), got.reshape(shape)
        mybit = (me_x // bit) & 1
        sent = pick(keep, 1 - mybit, 1) + pick(got, 1 - mybit, 1)
        keep = pick(keep, mybit, 1) + pick(got, mybit, 1)
        got = swap(sent, "gx", bit)
        bit *= 2
    total = keep + got
    row = pick(total, me_y, 0)
    for k in range(1, ny):
        row = row + swap(pick(total, me_y ^ k, 0), "gy", k)
    summed = row
    for k in range(1, ns):
        summed = summed + swap(row, "sa", k)
    parts = [summed] + [swap(summed, "gx", o) for o in range(1, nx)]
    gram_y = place_rows(where, parts, x_total * z_cells * s_total)
    return (gram_x, gram_y, core)


def solution(mesh):
    in_specs = (P(None, "sa", "gx", "gy"), P("gx", None), P("gy", None))
    out_specs = (P(("gx", "gy", "sa"), None), P("gy", None), P(None, "sa", "gx", "gy"))
    return jax.shard_map(
        local_step, mesh=mesh, in_specs=in_specs, out_specs=out_specs, check_vma=False
    )
```

```python
import functools
import math

import jax
import jax.numpy as jnp
from jax import lax
from jax.experimental import pallas as pl
from jax.experimental.pallas import tpu as pltpu
from jax.sharding import PartitionSpec as P


F32 = jnp.float32
BF16 = jnp.bfloat16
ROWS = (((0,), (0,)), ((), ()))
LANES = (((1,), (1,)), ((), ()))
PLAIN = (((1,), (0,)), ((), ()))


def swap(value, axis, offset):
    size = lax.axis_size(axis)
    return lax.ppermute(value, axis, [(i, i ^ offset) for i in range(size)])


def far_first(size):
    return [k for k in range(1, size) if k >= size // 2] + [k for k in range(1, size // 2)]


def early_shift(size):
    return size // 2


def pick(value, index, axis):
    return lax.dynamic_index_in_dim(value, index, axis, keepdims=False)


def split(value):
    high = value.astype(BF16)
    return high, (value - high.astype(F32)).astype(BF16)


def dot3(left, right, dims):
    (lc,), (rc,) = dims[0]
    lhs = jnp.concatenate([left[0], left[0], left[1]], axis=lc)
    rhs = jnp.concatenate([right[0], right[1], right[0]], axis=rc)
    return lax.dot_general(lhs, rhs, dims, preferred_element_type=F32)


def params():
    return pltpu.CompilerParams(vmem_limit_bytes=48 << 20)


def piece_sizes(own):
    sizes = (own // 4,) * 4
    assert all(n > 0 and n % 2 == 0 for n in sizes)
    return sizes, ((0,), (1,), (2,), (3,)), ((0, 1), (2,), (3,))


def in_hbm(arrays):
    return [pltpu.with_memory_space_constraint(a, pltpu.HBM) for a in arrays]


def whole_spec(shape):
    return pl.BlockSpec(shape, lambda i, s: (0,) * len(shape))


def cut_kernel(s_ref, *refs):
    half = len(refs) // 2
    for source, target in zip(refs[:half], refs[half:]):
        target[...] = source[...]


def cut(where, flat, pieces):
    unit = math.gcd(*[n for _, _, *counts in pieces for n in counts if n])
    block = (unit,) + flat.shape[1:]
    steps = max(size for *_, size in pieces) // unit
    in_specs, out_specs, out_shape = [], [], []
    for axis, k, own, start, size in pieces:

        def source(i, s, axis=axis, k=k, own=own, start=start, size=size):
            first = ((s[axis] ^ k) * own + start) // unit
            return (first + jnp.minimum(i, size // unit - 1), 0, 0)

        def target(i, s, size=size):
            return (jnp.minimum(i, size // unit - 1), 0, 0)

        in_specs.append(pl.BlockSpec(block, source))
        out_specs.append(pl.BlockSpec(block, target))
        out_shape.append(jax.ShapeDtypeStruct((size,) + flat.shape[1:], F32))
    return pl.pallas_call(
        cut_kernel,
        grid_spec=pltpu.PrefetchScalarGridSpec(
            num_scalar_prefetch=1, grid=(steps,), in_specs=in_specs, out_specs=out_specs
        ),
        out_shape=out_shape,
        cost_estimate=pl.CostEstimate(flops=1000, bytes_accessed=1 << 22, transcendentals=0),
    )(where, *[flat] * len(pieces))


def reverse_bits(value, count):
    bits = count.bit_length() - 1
    return sum(((value >> i) & 1) << (bits - 1 - i) for i in range(bits))


def rows_kernel(terms, s_ref, *refs):
    parts, out_ref = refs[:-1], refs[-1]
    size = parts[0].shape[0]
    for o, part in enumerate(parts):
        place = reverse_bits(s_ref[0] ^ o, len(parts))
        out_ref[pl.ds(pl.multiple_of(place * size, size), size), :] = part[...] / terms


def place_rows(where, parts, terms):
    size, width = parts[0].shape
    shape = (len(parts) * size, width)
    return pl.pallas_call(
        functools.partial(rows_kernel, terms),
        grid_spec=pltpu.PrefetchScalarGridSpec(
            num_scalar_prefetch=1,
            grid=(1,),
            in_specs=[whole_spec((size, width))] * len(parts),
            out_specs=whole_spec(shape),
        ),
        out_shape=jax.ShapeDtypeStruct(shape, F32),
        compiler_params=params(),
        cost_estimate=pl.CostEstimate(flops=1000, bytes_accessed=1 << 19, transcendentals=0),
    )(where, *parts)


def fy_kernel(ny, nx, s_ref, own_ref, *refs):
    pieces, (high_ref, low_ref, scratch) = refs[:nx], refs[nx:]
    depth = own_ref.shape[0]
    small = depth // nx
    scratch[pl.ds(pl.multiple_of(s_ref[1] * depth, depth), depth), :] = own_ref[...]
    for o in range(nx):
        for k in range(1, ny):
            start = (s_ref[1] ^ k) * depth + (s_ref[0] ^ o) * small
            scratch[pl.ds(pl.multiple_of(start, small), small), :] = pieces[o][k - 1]
    high_ref[...], low_ref[...] = split(scratch[...])


def gather_fy(sizes, where, factor_y, pieces):
    nx, ny = sizes[:2]
    depth, rank = factor_y.shape
    shape = (ny * depth, rank)
    return pl.pallas_call(
        functools.partial(fy_kernel, ny, nx),
        grid_spec=pltpu.PrefetchScalarGridSpec(
            num_scalar_prefetch=1,
            grid=(1,),
            in_specs=[whole_spec(factor_y.shape)] + [whole_spec(p.shape) for p in pieces],
            out_specs=[whole_spec(shape)] * 2,
            scratch_shapes=[pltpu.VMEM(shape, F32)],
        ),
        out_shape=[jax.ShapeDtypeStruct(shape, BF16)] * 2,
        compiler_params=params(),
        cost_estimate=pl.CostEstimate(flops=1000, bytes_accessed=1 << 20, transcendentals=0),
    )(where, factor_y, *pieces)


def chunk_kernel(sizes, count, first, last, s_ref, *refs):
    nx, ny, _ = sizes
    fields, refs = refs[: count * ny], refs[count * ny :]
    (fyh_ref, fyl_ref, fxt_ref), refs = refs[:3], refs[3:]
    if not first:
        gin_ref, refs = refs[0], refs[1:]
    keep_ref, sent_ref, refs = refs[0], refs[1], refs[2:]
    if last:
        gkeep_ref, gsent_ref, wide_ref, gram_ref = refs
    else:
        gram_ref, wide_ref = refs
    _, x_local, y_local = fields[0].shape
    me_x, me_y = s_ref[0], s_ref[1]
    n = wide_ref.shape[0] // x_local
    for k in range(ny):
        start = pl.multiple_of((me_y ^ k) * y_local, y_local)
        row = 0
        for p in range(count):
            part = fields[p * ny + k]
            rows = part.shape[0] * x_local
            wide_ref[row : row + rows, pl.ds(start, y_local)] = part[...].reshape(rows, y_local)
            row += rows
    wide = split(wide_ref[...])
    gram = dot3(wide, wide, ROWS)
    gram_ref[...] = gram if first else gin_ref[...] + gram

    half = dot3(wide, (fyh_ref[...], fyl_ref[...]), PLAIN)
    b_block = half.shape[1] // ny
    paired = jnp.concatenate(
        [
            half[p * x_local : (p + 1) * x_local, q * b_block : (q + 1) * b_block]
            for j in range(n // 2)
            for q in range(ny)
            for p in (2 * j, 2 * j + 1)
        ],
        axis=1,
    )
    a_block = fxt_ref.shape[0] // nx
    fx = jnp.concatenate(
        [
            fxt_ref[pl.ds(pl.multiple_of((me_x ^ o) * a_block, a_block), a_block), :]
            for o in range(nx)
        ],
        axis=0,
    )
    full = dot3(split(fx), split(paired), PLAIN)
    lanes = 2 * b_block
    for o in range(nx):
        target = sent_ref if o % 2 else keep_ref
        for j in range(n // 2):
            for q in range(ny):
                at = (j * ny + q) * lanes
                target[o // 2, q, j] = full[o * a_block : (o + 1) * a_block, at : at + lanes]
    if last:
        part = y_local // 2
        bit = me_x & 1
        for k in range(ny):
            mine = pl.multiple_of(k * y_local + bit * part, part)
            other = pl.multiple_of(k * y_local + (1 - bit) * part, part)
            gkeep_ref[k] = gram_ref[pl.ds(mine, part), :]
            gsent_ref[k] = gram_ref[pl.ds(other, part), :]


def chunk_terms(sizes, where, parts, fy, fxt, gram, last):
    nx, ny, _ = sizes
    _, x_local, y_local = parts[0].shape
    count = len(parts) // ny
    n = sum(part.shape[0] for part in parts[::ny])
    rank = fxt.shape[0]
    pairs = n // 2
    width = ny * y_local
    a_block, b_block = rank // nx, rank // ny
    half = (nx // 2, ny, pairs, a_block, 2 * b_block)
    specs = [whole_spec(part.shape) for part in parts]
    specs += [whole_spec(fy[0].shape)] * 2 + [whole_spec(fxt.shape)]
    args = [*in_hbm(parts), *fy, fxt]
    first = gram is None
    if not first:
        specs.append(whole_spec((width, width)))
        args += in_hbm([gram])
    out_specs = [whole_spec(half)] * 2
    out_shape = [jax.ShapeDtypeStruct(half, F32)] * 2
    scratch = [pltpu.VMEM((n * x_local, width), F32)]
    if last:
        gshape = (ny, y_local // 2, width)
        out_specs += [whole_spec(gshape)] * 2
        out_shape += [jax.ShapeDtypeStruct(gshape, F32)] * 2
        scratch.append(pltpu.VMEM((width, width), F32))
    else:
        out_specs.append(whole_spec((width, width)))
        out_shape.append(pltpu.HBM((width, width), F32))
    flops = 2 * n * x_local * (width * width + width * rank + rank * rank) * 3
    return pl.pallas_call(
        functools.partial(chunk_kernel, sizes, count, first, last),
        grid_spec=pltpu.PrefetchScalarGridSpec(
            num_scalar_prefetch=1,
            grid=(1,),
            in_specs=specs,
            out_specs=out_specs,
            scratch_shapes=scratch,
        ),
        out_shape=out_shape,
        compiler_params=params(),
        cost_estimate=pl.CostEstimate(flops=flops, bytes_accessed=1 << 22, transcendentals=0),
    )(where, *args)


def gram_x_kernel(sizes, s_ref, *refs):
    nx = sizes[0]
    fields, (keep_ref, sent_ref, tall_ref, gram_ref) = refs[:nx], refs[nx:]
    pair, x_local, y_local = fields[0].shape
    me_x = s_ref[0]
    for o in range(nx):
        start = pl.multiple_of((me_x ^ o) * x_local, x_local)
        for p in range(pair):
            tall_ref[pl.ds(start, x_local), p * y_local : (p + 1) * y_local] = fields[o][p]
    tall = split(tall_ref[...])
    gram = dot3(tall, tall, LANES)
    step = pl.program_id(0)

    @pl.when(step == 0)
    def _():
        gram_ref[...] = gram

    @pl.when(step > 0)
    def _():
        gram_ref[...] += gram

    @pl.when(step == pl.num_programs(0) - 1)
    def _():
        bit = me_x & 1
        for j in range(nx // 2):
            mine = pl.multiple_of((2 * j + bit) * x_local, x_local)
            other = pl.multiple_of((2 * j + 1 - bit) * x_local, x_local)
            keep_ref[j] = gram_ref[pl.ds(mine, x_local), :]
            sent_ref[j] = gram_ref[pl.ds(other, x_local), :]


def gram_x_terms(sizes, where, flat, parts):
    nx = sizes[0]
    own, x_local, y_local = parts[0].shape
    width = nx * x_local
    batch = 4
    field = (batch, x_local, y_local)
    specs = [pl.BlockSpec(field, lambda i, s: (s[0] * own // batch + i, 0, 0))]
    specs += [pl.BlockSpec(field, lambda i, s: (i, 0, 0))] * (nx - 1)
    half = (nx // 2, x_local, width)
    flops = 2 * own * y_local * width * width * 3
    return pl.pallas_call(
        functools.partial(gram_x_kernel, sizes),
        grid_spec=pltpu.PrefetchScalarGridSpec(
            num_scalar_prefetch=1,
            grid=(own // batch,),
            in_specs=specs,
            out_specs=[whole_spec(half)] * 2,
            scratch_shapes=[pltpu.VMEM((width, batch * y_local), F32), pltpu.VMEM((width, width), F32)],
        ),
        out_shape=[jax.ShapeDtypeStruct(half, F32)] * 2,
        compiler_params=params(),
        cost_estimate=pl.CostEstimate(flops=flops, bytes_accessed=1 << 23, transcendentals=0),
    )(where, *in_hbm([flat, *parts]))


def pack_kernel(ny, extra, s_ref, *refs):
    outs, refs = refs[-ny:], refs[:-ny]
    if extra:
        xrows, refs = refs[-1], refs[:-1]
    lanes = outs[0].shape[2]
    for k in range(ny):
        at = s_ref[1] ^ k
        row = 0
        for keep, got in zip(refs[::2], refs[1::2]):
            outs[k][row : row + keep.shape[1]] = keep[at] + got[at]
            row += keep.shape[1]
        if extra:
            size = xrows.shape[1]
            for j in range(xrows.shape[2] // lanes):
                block, start = divmod(j * size, outs[k].shape[1])
                outs[k][row + block, start : start + size] = xrows[
                    at, :, j * lanes : (j + 1) * lanes
                ]


def pack(sizes, where, halves, xrows=None):
    ny = sizes[1]
    args = [v for pair in halves for v in pair]
    _, _, a_block, lanes = args[0].shape
    count = sum(v.shape[1] for v in args[::2])
    if xrows is not None:
        args.append(xrows)
        count += xrows.shape[1] * xrows.shape[2] // (a_block * lanes)
    shape = (count, a_block, lanes)
    return pl.pallas_call(
        functools.partial(pack_kernel, ny, xrows is not None),
        grid_spec=pltpu.PrefetchScalarGridSpec(
            num_scalar_prefetch=1,
            grid=(1,),
            in_specs=[whole_spec(a.shape) for a in args],
            out_specs=[whole_spec(shape)] * ny,
        ),
        out_shape=[jax.ShapeDtypeStruct(shape, F32)] * ny,
        compiler_params=params(),
        cost_estimate=pl.CostEstimate(flops=1000, bytes_accessed=1 << 20, transcendentals=0),
    )(where, *args)


def unpack_kernel(ny, own, starts, counts, terms, s_ref, *refs):
    parts, (out_ref, gram_ref) = refs[:-2], refs[-2:]
    b_block = out_ref.shape[2]
    for c, start in enumerate(starts):
        for k in range(ny):
            part = parts[c * ny + k]
            for j in range(counts[c] // 2):
                base = (s_ref[1] ^ k) * own + start + 2 * j
                out_ref[base] = part[j, :, :b_block]
                out_ref[base + 1] = part[j, :, b_block:]
    size, lanes = gram_ref.shape[0], 2 * b_block
    for j in range(gram_ref.shape[1] // lanes):
        block, start = divmod(j * size, out_ref.shape[1])
        total = parts[0][counts[0] // 2 + block, start : start + size]
        for k in range(1, ny):
            total = total + parts[k][counts[0] // 2 + block, start : start + size]
        gram_ref[:, j * lanes : (j + 1) * lanes] = total / terms


def unpack(sizes, where, parts, starts, counts, rows, gram_shape, terms):
    ny = sizes[1]
    _, a_block, lanes = parts[0].shape
    shape = (rows, a_block, lanes // 2)
    return pl.pallas_call(
        functools.partial(unpack_kernel, ny, rows // ny, starts, counts, terms),
        grid_spec=pltpu.PrefetchScalarGridSpec(
            num_scalar_prefetch=1,
            grid=(1,),
            in_specs=[whole_spec(p.shape) for p in parts],
            out_specs=[whole_spec(shape), whole_spec(gram_shape)],
        ),
        out_shape=[jax.ShapeDtypeStruct(shape, F32), jax.ShapeDtypeStruct(gram_shape, F32)],
        compiler_params=params(),
        cost_estimate=pl.CostEstimate(flops=1000, bytes_accessed=3 << 20, transcendentals=0),
    )(where, *parts)


def local_step(slab, factor_x, factor_y):
    z_cells, s_local, x_local, y_local = slab.shape
    sizes = nx, ny, ns = tuple(lax.axis_size(a) for a in ("gx", "gy", "sa"))
    me_x, me_y, me_s = (lax.axis_index(a) for a in ("gx", "gy", "sa"))
    where = jnp.stack([me_x, me_y, me_s]).astype(jnp.int32)
    rank = factor_x.shape[1]
    a_block, b_block = rank // nx, rank // ny
    rows = z_cells * s_local
    flat = slab.reshape((rows, x_local, y_local))
    own_y, own_x = rows // ny, rows // nx
    counts, chunks, sends = piece_sizes(own_y)
    starts = [sum(counts[:c]) for c in range(len(counts))]
    x_total, y_total, s_total = x_local * nx, y_local * ny, s_local * ns

    keys = [[(1, k, own_y, starts[c], counts[c]) for k in range(ny)] for c in range(len(counts))]
    x_keys = [(0, k, own_x, 0, own_x) for k in range(1, nx)]
    own_keys = [key[0] for key in keys]
    early = early_shift(nx)
    first = far_first(ny)[0]
    groups = [[keys[0][first]], [x_keys[early - 1]] + [key for key in keys[0][1:] if key[1] != first]]
    groups += [keys[1][1:] + own_keys[:2]]
    groups += [keys[2] + keys[3], [key for key in x_keys if key[1] != early]]
    pieces = {}
    for group in groups:
        pieces.update(zip(group, cut(where, flat, group)))
    along_y = []
    for c in range(len(counts)):
        here = [pieces[keys[c][0]]]
        here += [swap(pieces[keys[c][k]], "gy", k) for k in range(1, ny)]
        along_y.append(here)
    along_x = [swap(pieces[x_keys[k - 1]], "gx", k) for k in range(1, nx)]
    mine = pick(factor_y.reshape((nx, y_local // nx, rank)), me_x, 0)
    crossed = jnp.stack([swap(mine, "gy", k) for k in range(1, ny)])
    fy_parts = [crossed] + [swap(crossed, "gx", o) for o in range(1, nx)]
    fy = gather_fy(sizes, where, factor_y, fy_parts)
    fxt = factor_x.T

    gram = None
    core_parts, reduced = [], []
    for c, members in enumerate(chunks):
        last = c == len(chunks) - 1
        parts = sum((along_y[p] for p in members), [])
        out = chunk_terms(sizes, where, parts, fy, fxt, gram, last)
        keep, sent, gram = out[0], out[1], out[2:]
        if last:
            gkeep, gsent = gram
            ggot = swap(gsent, "gx", 1)
        else:
            gram = gram[0]
        bit = 1
        while bit < nx:
            got = swap(sent, "gx", bit)
            if 2 * bit < nx:
                sent = keep[1::2] + got[1::2]
                keep, got = keep[0::2], got[0::2]
                keep = keep + got
            bit *= 2
        reduced.append((keep[0], got[0]))
    keep, sent = gram_x_terms(sizes, where, flat, along_x)
    got = swap(sent, "gx", 1)
    bit = 2
    while bit < nx:
        keep = keep.reshape((-1, 2, x_local, x_total))
        got = got.reshape((-1, 2, x_local, x_total))
        mybit = (me_x // bit) & 1
        sent = pick(keep, 1 - mybit, 1) + pick(got, 1 - mybit, 1)
        keep = pick(keep, mybit, 1) + pick(got, mybit, 1)
        got = swap(sent, "gx", bit)
        bit *= 2
    halves = [v[0].reshape((ny, ns, -1, x_total)) for v in (keep, got)]

    def sa_rows(k):
        return pick(halves[0], me_s ^ k, 1) + pick(halves[1], me_s ^ k, 1)

    x_rows = sa_rows(0)
    for k in range(1, ns):
        x_rows = x_rows + swap(sa_rows(k), "sa", k)

    for c, members in enumerate(sends):
        z_parts = pack(sizes, where, [reduced[m] for m in members], None if c else x_rows)
        core_parts += [swap(z_parts[k], "gy", k) if k else z_parts[0] for k in range(ny)]
    send_starts = [starts[chunks[m[0]][0]] for m in sends]
    send_counts = [sum(counts[p] for m in members for p in chunks[m]) for members in sends]
    gram_shape = x_rows.shape[1:]
    terms = y_total * z_cells * s_total
    core, gram_x = unpack(
        sizes, where, core_parts, send_starts, send_counts, rows, gram_shape, terms
    )
    core = core.reshape((z_cells, s_local, a_block, b_block))

    keep, got = gkeep, ggot
    bit = 2
    while bit < nx:
        shape = (ny, 2, keep.shape[1] // 2, y_total)
        keep, got = keep.reshape(shape), got.reshape(shape)
        mybit = (me_x // bit) & 1
        sent = pick(keep, 1 - mybit, 1) + pick(got, 1 - mybit, 1)
        keep = pick(keep, mybit, 1) + pick(got, mybit, 1)
        got = swap(sent, "gx", bit)
        bit *= 2

    def gy_rows(k):
        return pick(keep, me_y ^ k, 0) + pick(got, me_y ^ k, 0)

    row = gy_rows(0)
    for k in range(1, ny):
        row = row + swap(gy_rows(k), "gy", k)
    summed = row
    for k in range(1, ns):
        summed = summed + swap(row, "sa", k)
    parts = [summed] + [swap(summed, "gx", o) for o in range(1, nx)]
    gram_y = place_rows(where, parts, x_total * z_cells * s_total)
    return (gram_x, gram_y, core)


def solution(mesh):
    in_specs = (P(None, "sa", "gx", "gy"), P("gx", None), P("gy", None))
    out_specs = (P(("gx", "gy", "sa"), None), P("gy", None), P(None, "sa", "gx", "gy"))
    return jax.shard_map(
        local_step, mesh=mesh, in_specs=in_specs, out_specs=out_specs, check_vma=False
    )
```
